32 devices in a mesh: vel: 4 (over x, core), gx: 4 (over z), gy: 2 (over y).
Axes of the slice: x: 2, y: 2, z: 4, core: 2. Of those that a mesh axis runs over, the one named last changes fastest.
Arguments:
- previous: bfloat16 [4096, 32, 256], P('vel', 'gx', 'gy'), may hold values from 0 to 4, as said below
- relax_time: float32 [32, 256], P('gx', 'gy'), may hold values from 0.05 to 20
- left_right_kind: int32 [2, 256], P(None, 'gy'), may hold values from 0 to 1
- bottom_top_kind: int32 [2, 32], P(None, 'gx'), may hold values from 0 to 1
- left_right_inflow: bfloat16 [4096, 2, 256], P('vel', None, 'gy'), may hold values from 0.049804688 to 1
- bottom_top_inflow: bfloat16 [4096, 2, 32], P('vel', None, 'gx'), may hold values from 0.049804688 to 1
Outputs:
- updated: bfloat16 [4096, 32, 256], P('vel', 'gx', 'gy')
The draws below stay inside these ranges and needn't reach their ends.
Inputs may be any that keep to these rules, and one draw needn't show every extreme that they name: previous is positive in every entry. `left_right_kind`: 1 marks an inflow edge cell, 0 a diffuse wall. `bottom_top_kind`: 1 marks an inflow edge cell, 0 a diffuse wall.
All inputs are finite; a program needn't handle non-finite values.
Results may differ from the reference program's by a relative error of at most 0.0042.
Values may be sent and summed in bfloat16 or wider, within the bound.
No kernel may reach another device: no remote copies, remote signals or barrier semaphores. Data moves between devices by JAX's collectives and lax.ppermute only.
A program may use at most 128 MiB of HBM per device.

```python
import math
import jax
import jax.numpy as jnp
from jax import lax

NVX = 64
V = 4096
NEWTON = 2
SWEEPS = 4
HORIZONTAL_CELLS = 32
VERTICAL_CELLS = 256


def draw_previous(key, part):
    random_seeds = jax.random.split(jax.random.fold_in(key, 11), 10)
    peak = jax.random.uniform(random_seeds[0], (1, HORIZONTAL_CELLS, VERTICAL_CELLS), jnp.float32, 0.5, 2.0)
    cool_x = jax.random.uniform(random_seeds[1], (1, HORIZONTAL_CELLS, VERTICAL_CELLS), jnp.float32, -1.2, 1.2)
    cool_y = jax.random.uniform(random_seeds[2], (1, HORIZONTAL_CELLS, VERTICAL_CELLS), jnp.float32, -1.2, 1.2)
    chilly_thermal_level = jax.random.uniform(random_seeds[3], (1, HORIZONTAL_CELLS, VERTICAL_CELLS), jnp.float32, 1.0, 3.0)
    hotspot_indicator = jax.random.randint(random_seeds[5], (1, HORIZONTAL_CELLS, VERTICAL_CELLS), 0, 2) == 1
    sign_x = (2 * jax.random.randint(random_seeds[6], (1, HORIZONTAL_CELLS, VERTICAL_CELLS), 0, 2) - 1).astype(jnp.float32)
    sign_y = (2 * jax.random.randint(random_seeds[7], (1, HORIZONTAL_CELLS, VERTICAL_CELLS), 0, 2) - 1).astype(jnp.float32)
    hot_x = sign_x * jax.random.uniform(random_seeds[8], (1, HORIZONTAL_CELLS, VERTICAL_CELLS), jnp.float32, 1.8, 2.8)
    hot_y = sign_y * jax.random.uniform(random_seeds[9], (1, HORIZONTAL_CELLS, VERTICAL_CELLS), jnp.float32, 1.8, 2.8)
    tepid_thermal_level = jax.random.uniform(jax.random.fold_in(random_seeds[3], 5), (1, HORIZONTAL_CELLS, VERTICAL_CELLS), jnp.float32, 4.0, 8.0)
    drift_horizontal = jnp.where(hotspot_indicator, hot_x, cool_x)
    drift_vertical = jnp.where(hotspot_indicator, hot_y, cool_y)
    pointwise_thermal_state = jnp.where(hotspot_indicator, tepid_thermal_level, chilly_thermal_level)
    rough = jnp.clip(1.0 + 0.25 * jax.random.normal(random_seeds[4], (V, HORIZONTAL_CELLS, VERTICAL_CELLS), jnp.float32), 0.4, 1.6)
    spacing = 12.0 / NVX
    vel_index = jnp.arange(V, dtype=jnp.int32)
    lattice_abscissa_horizontal = (((vel_index % NVX).astype(jnp.float32) - (NVX - 1) / 2.0) * spacing).reshape(V, 1, 1)
    lattice_abscissa_vertical = (((vel_index // NVX).astype(jnp.float32) - (NVX - 1) / 2.0) * spacing).reshape(V, 1, 1)
    normal_curve_power = -((lattice_abscissa_horizontal - drift_horizontal) ** 2 + (lattice_abscissa_vertical - drift_vertical) ** 2) / (2.0 * pointwise_thermal_state)
    return (peak * jnp.exp(normal_curve_power) * rough).astype(jnp.bfloat16)


def touch_ends(array, stream_key, smallest, high):
    dims = array.shape
    spot = [jax.random.randint(jax.random.fold_in(stream_key, axis), (), 0, dims[axis]) for axis in range(len(dims))]
    array = array.at[tuple(spot)].set(smallest)
    longest = dims.index(max(dims))
    spot[longest] = (spot[longest] + 1) % dims[longest]
    return array.at[tuple(spot)].set(high)


def steps_of(own_key, dims, pieces, smallest, largest):
    loudness = 1.0
    for axis_at, shards_of in pieces:
        heights = jax.random.uniform(jax.random.fold_in(jax.random.fold_in(own_key, 6), axis_at), (shards_of,), jnp.float32, smallest / len(pieces), largest / len(pieces))
        loudness = loudness * jnp.repeat(jnp.exp(heights), dims[axis_at] // shards_of).reshape((-1,) + (1,) * (len(dims) - 1 - axis_at))
    return loudness


def setup_inputs(seed: int = 0) -> dict:
    arg_keys = jax.random.split(jax.random.key(seed), 7)
    return {
        "previous": draw_previous(jax.random.fold_in(arg_keys[6], 71), 0),
        "relax_time": jnp.clip(jnp.exp(math.log(20.0) - 5.9914645 * jax.random.uniform(arg_keys[1], (HORIZONTAL_CELLS, VERTICAL_CELLS), jnp.float32) ** steps_of(arg_keys[1], (HORIZONTAL_CELLS, VERTICAL_CELLS), ((0, 4), (1, 2)), -0.2, 0.2)), 0.05, 20.0),
        "left_right_kind": touch_ends(jax.random.randint(arg_keys[2], (2, VERTICAL_CELLS), 0, 2), jax.random.fold_in(arg_keys[2], 1), 0, 1).astype(jnp.int32),
        "bottom_top_kind": touch_ends(jax.random.randint(arg_keys[3], (2, HORIZONTAL_CELLS), 0, 2), jax.random.fold_in(arg_keys[3], 1), 0, 1).astype(jnp.int32),
        "left_right_inflow": jnp.clip(0.049804688 + 0.9501953 * jax.random.uniform(arg_keys[4], (V, 2, VERTICAL_CELLS), jnp.float32) ** steps_of(arg_keys[4], (V, 2, VERTICAL_CELLS), ((0, 4), (2, 2)), -0.2, 0.2), 0.049804688, 1.0).astype(jnp.bfloat16),
        "bottom_top_inflow": jnp.clip(0.049804688 + 0.9501953 * jax.random.uniform(arg_keys[5], (V, 2, HORIZONTAL_CELLS), jnp.float32) ** steps_of(arg_keys[5], (V, 2, HORIZONTAL_CELLS), ((0, 4), (2, 4)), -0.2, 0.2), 0.049804688, 1.0).astype(jnp.bfloat16),
    }


courant = 100.0


def velocity_grid(first_vel, vel_count):
    spacing = 12.0 / NVX
    vel_index = first_vel + jnp.arange(vel_count, dtype=jnp.int32)
    lattice_abscissa_horizontal = ((vel_index % NVX).astype(jnp.float32) - (NVX - 1) / 2.0) * spacing
    lattice_abscissa_vertical = ((vel_index // NVX).astype(jnp.float32) - (NVX - 1) / 2.0) * spacing
    return lattice_abscissa_horizontal, lattice_abscissa_vertical


def basis_rows(lattice_abscissa_horizontal, lattice_abscissa_vertical, weight):
    energy = (lattice_abscissa_horizontal * lattice_abscissa_horizontal + lattice_abscissa_vertical * lattice_abscissa_vertical) / 2.0
    ones_row = jnp.ones_like(lattice_abscissa_horizontal)
    moment_basis = jnp.stack([ones_row, lattice_abscissa_horizontal, lattice_abscissa_vertical, energy]) * weight
    product_basis = jnp.stack([ones_row, lattice_abscissa_horizontal, lattice_abscissa_vertical, energy, lattice_abscissa_horizontal * lattice_abscissa_horizontal, lattice_abscissa_horizontal * lattice_abscissa_vertical, lattice_abscissa_horizontal * energy,
                               lattice_abscissa_vertical * lattice_abscissa_vertical, lattice_abscissa_vertical * energy, energy * energy]) * weight
    return moment_basis, product_basis


def equilibrium(params, lattice_abscissa_horizontal, lattice_abscissa_vertical):
    energy = (lattice_abscissa_horizontal * lattice_abscissa_horizontal + lattice_abscissa_vertical * lattice_abscissa_vertical) / 2.0
    normal_curve_power = (params[0][None, :] + lattice_abscissa_horizontal[:, None] * params[1][None, :]
                + lattice_abscissa_vertical[:, None] * params[2][None, :] + energy[:, None] * params[3][None, :])
    return jnp.exp(normal_curve_power)


def start_params(integral_statistics):
    particle_concentration = integral_statistics[0]
    mean_flow_horizontal = integral_statistics[1] / particle_concentration
    mean_flow_vertical = integral_statistics[2] / particle_concentration
    kinetic_norm_square = mean_flow_horizontal * mean_flow_horizontal + mean_flow_vertical * mean_flow_vertical
    pointwise_thermal_state = integral_statistics[3] / particle_concentration - kinetic_norm_square / 2.0
    return jnp.stack([jnp.log(particle_concentration / pointwise_thermal_state) - kinetic_norm_square / (2.0 * pointwise_thermal_state),
                      mean_flow_horizontal / pointwise_thermal_state, mean_flow_vertical / pointwise_thermal_state, -1.0 / pointwise_thermal_state])


def solve_four(hessian, gradient):
    matrix = [list(row_list) for row_list in hessian]
    target = list(gradient)
    for pivot in range(4):
        for lower in range(pivot + 1, 4):
            factor = matrix[lower][pivot] / matrix[pivot][pivot]
            for column_at in range(pivot, 4):
                matrix[lower][column_at] = matrix[lower][column_at] - factor * matrix[pivot][column_at]
            target[lower] = target[lower] - factor * target[pivot]
    result = [None, None, None, None]
    for pivot in (3, 2, 1, 0):
        accum = target[pivot]
        for column_at in range(pivot + 1, 4):
            accum = accum - matrix[pivot][column_at] * result[column_at]
        result[pivot] = accum / matrix[pivot][pivot]
    return result


def newton_update(params, partials, integral_statistics):
    layout = [[0, 1, 2, 3], [1, 4, 5, 6], [2, 5, 7, 8], [3, 6, 8, 9]]
    gradient = [partials[place] - integral_statistics[place] for place in range(4)]
    hessian = [[partials[layout[row_at][column_at]] for column_at in range(4)] for row_at in range(4)]
    correction = solve_four(hessian, gradient)
    return params - jnp.stack(correction)


def reference(previous, relax_time, left_right_kind, bottom_top_kind, left_right_inflow, bottom_top_inflow):
    spacing = 12.0 / NVX
    weight = spacing * spacing / (2.0 * math.pi)
    time_step = courant / ((NVX - 1) * spacing)
    lattice_abscissa_horizontal, lattice_abscissa_vertical = velocity_grid(0, V)
    moment_basis, product_basis = basis_rows(lattice_abscissa_horizontal, lattice_abscissa_vertical, weight)
    highest = lax.Precision.HIGHEST

    def row_source(row_item):
        column, relax_row = row_item
        integral_statistics = jnp.dot(moment_basis, column.astype(jnp.float32), precision=highest)
        params = start_params(integral_statistics)
        for number in range(NEWTON):
            partials = jnp.dot(product_basis, equilibrium(params, lattice_abscissa_horizontal, lattice_abscissa_vertical), precision=highest)
            params = newton_update(params, partials, integral_statistics)
        maxwell = equilibrium(params, lattice_abscissa_horizontal, lattice_abscissa_vertical)
        return column.astype(jnp.float32) / time_step + maxwell / relax_row[None, :]

    source = lax.map(row_source, (jnp.moveaxis(previous, 1, 0), relax_time))
    source = jnp.moveaxis(source, 0, 1)
    wall_all = jnp.exp(-(lattice_abscissa_horizontal * lattice_abscissa_horizontal + lattice_abscissa_vertical * lattice_abscissa_vertical) / 2.0)
    wall_norm = jnp.sum(jnp.maximum(lattice_abscissa_horizontal, 0.0) * wall_all) * weight
    pos_x = jnp.maximum(lattice_abscissa_horizontal, 0.0)[:, None, None]
    neg_x = jnp.maximum(-lattice_abscissa_horizontal, 0.0)[:, None, None]
    pos_y = jnp.maximum(lattice_abscissa_vertical, 0.0)[:, None, None]
    neg_y = jnp.maximum(-lattice_abscissa_vertical, 0.0)[:, None, None]
    denominator = 1.0 / time_step + 1.0 / relax_time[None, :, :] + (jnp.abs(lattice_abscissa_horizontal) + jnp.abs(lattice_abscissa_vertical))[:, None, None]
    out_left = jnp.maximum(-lattice_abscissa_horizontal, 0.0) * weight
    out_right = jnp.maximum(lattice_abscissa_horizontal, 0.0) * weight
    out_bottom = jnp.maximum(-lattice_abscissa_vertical, 0.0) * weight
    out_top = jnp.maximum(lattice_abscissa_vertical, 0.0) * weight
    current = previous
    for number in range(SWEEPS):
        values = current.astype(jnp.float32)
        flux_left = jnp.dot(out_left, values[:, 0, :], precision=highest)
        flux_right = jnp.dot(out_right, values[:, -1, :], precision=highest)
        flux_bottom = jnp.dot(out_bottom, values[:, :, 0], precision=highest)
        flux_top = jnp.dot(out_top, values[:, :, -1], precision=highest)
        ghost_left = jnp.where(left_right_kind[0][None, :] == 1, left_right_inflow[:, 0, :].astype(jnp.float32),
                               (flux_left / wall_norm)[None, :] * wall_all[:, None])
        ghost_right = jnp.where(left_right_kind[1][None, :] == 1, left_right_inflow[:, 1, :].astype(jnp.float32),
                                (flux_right / wall_norm)[None, :] * wall_all[:, None])
        ghost_bottom = jnp.where(bottom_top_kind[0][None, :] == 1, bottom_top_inflow[:, 0, :].astype(jnp.float32),
                                 (flux_bottom / wall_norm)[None, :] * wall_all[:, None])
        ghost_top = jnp.where(bottom_top_kind[1][None, :] == 1, bottom_top_inflow[:, 1, :].astype(jnp.float32),
                              (flux_top / wall_norm)[None, :] * wall_all[:, None])
        from_left = jnp.concatenate([ghost_left[:, None, :], values[:, :-1, :]], axis=1)
        from_right = jnp.concatenate([values[:, 1:, :], ghost_right[:, None, :]], axis=1)
        from_below = jnp.concatenate([ghost_bottom[:, :, None], values[:, :, :-1]], axis=2)
        from_above = jnp.concatenate([values[:, :, 1:], ghost_top[:, :, None]], axis=2)
        numerator = source + pos_x * from_left + neg_x * from_right + pos_y * from_below + neg_y * from_above
        current = (numerator / denominator).astype(jnp.bfloat16)
    return current
```

```python
import functools
import math

import jax
import jax.numpy as jnp
import numpy as np
from jax import lax
from jax.experimental import pallas as pl
from jax.experimental.pallas import tpu as pltpu
from jax.sharding import PartitionSpec as P

NVX = 64
HALF = NVX // 2
NEWTON = 2
SWEEPS = 4
COURANT = 100.0
STEP = 12.0 / NVX
UNIT = STEP / 2.0
WEIGHT = STEP * STEP / (2.0 * math.pi)
TIME_STEP = COURANT / ((NVX - 1) * STEP)
LANES = 128
HIGHEST = lax.Precision.HIGHEST
F32 = jnp.float32
BF16 = jnp.bfloat16


def wall_norm_value():
    line = (np.arange(NVX) - (NVX - 1) / 2.0) * STEP
    gauss = np.exp(-line * line / 2.0)
    return float(np.sum(np.maximum(line, 0.0) * gauss) * np.sum(gauss) * WEIGHT)


FLUX_SCALE = WEIGHT * UNIT / wall_norm_value()


def nn(a, b, precision=None):
    return lax.dot_general(a, b, (((1,), (0,)), ((), ())), precision=precision, preferred_element_type=F32)


def nt(a, b, precision=None):
    return lax.dot_general(a, b, (((1,), (1,)), ((), ())), precision=precision, preferred_element_type=F32)


def tn(a, b, precision=None):
    return lax.dot_general(a, b, (((0,), (0,)), ((), ())), precision=precision, preferred_element_type=F32)


def iota(shape, dim):
    return lax.broadcasted_iota(jnp.int32, shape, dim)


def lane_ints(first_ky, sign, start, shape):
    lane = iota(shape, len(shape) - 1) + start
    ix = 2 * (lane % HALF + HALF * sign) - (NVX - 1)
    iy = 2 * (first_ky + lane // HALF) - (NVX - 1)
    return ix, iy


def flip_matrix(up, size):
    row, col = iota((size, size), 0), iota((size, size), 1)
    return (col == jnp.where(up, row, size - 1 - row)).astype(F32)


def reverse_rows(a):
    return jnp.concatenate([a[i : i + 1] for i in range(a.shape[0] - 1, -1, -1)], axis=0)


def pieces(a):
    high = a.astype(BF16).astype(F32)
    rest = a - high
    middle = rest.astype(BF16).astype(F32)
    return [high, middle, rest - middle]


def moments_kernel(info, pt, pay, ymsg):
    cells_x, _, count, cells_y = pt.shape
    first_ky, up = info[0], info[1] == 1
    y_out = jnp.where(up, cells_y - 1, 0)
    row = iota((16, count), 0)
    weights = []
    for sign in range(2):
        ix, iy = lane_ints(first_ky, sign, 0, (16, count))
        energy = ix * ix + iy * iy
        low = energy % 64
        table = jnp.where(row == 0, 1, jnp.where(row == 1, ix, jnp.where(row == 2, iy, jnp.where(
            row == 3, energy - low, jnp.where(row == 4, low, jnp.where(row == 5, jnp.abs(ix), 0))))))
        weights.append(table.astype(F32).astype(BF16))
    edge = [jnp.zeros((16, count), F32) for _ in range(2)]
    out_row = [None, None]
    pick_row, pick_col = iota((16, cells_y), 0), iota((16, cells_y), 1)
    for x in range(cells_x):
        total = None
        for sign in range(2):
            block = pt[x, sign]
            part = nn(weights[sign], block)
            if x == (cells_x - 1) * sign:
                out_row[sign] = part[5:6]
            total = part if total is None else total + part
            at = x if sign else cells_x - 1 - x
            pick = ((pick_row == at) & (pick_col == y_out)).astype(F32).astype(BF16)
            edge[sign] = edge[sign] + nt(pick, block)
        pay[0, x : x + 1, :] = total[0:1]
        pay[1, x : x + 1, :] = total[1:2]
        pay[2, x : x + 1, :] = total[2:3]
        pay[3, x : x + 1, :] = total[3:4] + total[4:5]
    flip = flip_matrix(up, cells_y)
    fx = jnp.concatenate([out_row[0], out_row[1], jnp.zeros((6, cells_y), F32)], axis=0)
    pay[4] = nt(fx, flip, HIGHEST)
    for sign in range(2):
        total = jnp.zeros((cells_x, LANES), F32)
        for at in range(count // LANES):
            _, iy = lane_ints(first_ky, sign, at * LANES, (cells_x, LANES))
            total += jnp.abs(iy).astype(F32) * edge[sign][:cells_x, at * LANES : (at + 1) * LANES]
        pay[6 - sign] = total
        ymsg[sign] = edge[sign][:cells_x].astype(BF16)


def newton_params(u0, u1, u2, u3):
    ux, uy = u1 / u0, u2 / u0
    square = ux * ux + uy * uy
    temperature = u3 / u0 - square / 2.0
    p = [jnp.log(u0 / temperature) - square / (2.0 * temperature), ux / temperature, uy / temperature, -1.0 / temperature]
    line = [float((i - (NVX - 1) / 2.0) * STEP) for i in range(NVX)]
    for _ in range(NEWTON):
        half_p3 = p[3] * 0.5
        sums, tops = [], []
        for slope in (p[1], p[2]):
            top = None
            for value in line:
                arg = value * (slope + value * half_p3)
                top = arg if top is None else jnp.maximum(top, arg)
            total = [None] * 5
            for value in line:
                term = jnp.exp(value * (slope + value * half_p3) - top)
                for power in range(5):
                    total[power] = term if total[power] is None else total[power] + term
                    term = term * value
            sums.append(total)
            tops.append(top)
        scale = jnp.exp(p[0] + (tops[0] + tops[1])) * WEIGHT
        x = sums[0]
        y = [scale * t for t in sums[1]]
        x2, y2 = x[2] * y[0], x[0] * y[2]
        n = [x[0] * y[0], x[1] * y[0], x[0] * y[1], (x2 + y2) * 0.5, x2, x[1] * y[1],
             (x[3] * y[0] + x[1] * y[2]) * 0.5, y2, (x[2] * y[1] + x[0] * y[3]) * 0.5,
             (x[4] * y[0] + 2.0 * (x[2] * y[2]) + x[0] * y[4]) * 0.25]
        layout = [[0, 1, 2, 3], [1, 4, 5, 6], [2, 5, 7, 8], [3, 6, 8, 9]]
        matrix = [[n[layout[r][c]] for c in range(4)] for r in range(4)]
        target = [n[0] - u0, n[1] - u1, n[2] - u2, n[3] - u3]
        for pivot in range(4):
            for lower in range(pivot + 1, 4):
                factor = matrix[lower][pivot] / matrix[pivot][pivot]
                for col in range(pivot, 4):
                    matrix[lower][col] = matrix[lower][col] - factor * matrix[pivot][col]
                target[lower] = target[lower] - factor * target[pivot]
        result = [None] * 4
        for pivot in (3, 2, 1, 0):
            accum = target[pivot]
            for col in range(pivot + 1, 4):
                accum = accum - matrix[pivot][col] * result[col]
            result[pivot] = accum / matrix[pivot][pivot]
        p = [a - b for a, b in zip(p, result)]
    return p


def block_speeds(first_ky, block, per_sign, shape):
    ix, iy = lane_ints(first_ky, block // per_sign, (block % per_sign) * LANES, shape)
    return jnp.abs(ix).astype(F32) * UNIT, jnp.abs(iy).astype(F32) * UNIT


def fill_inflow(info, kindy, flux, g, xin, yin, xw, yw, kx):
    blocks, slots, padded, _ = g.shape
    cells_x, cells_y = slots - 1, padded - 8
    per_sign = blocks // 2
    first_ky, up = info[0], info[1] == 1
    devices = flux.shape[0]
    lo = [sum(flux[d, at] for d in range(devices // 2)) for at in range(3)]
    hi = [sum(flux[d, at] for d in range(devices // 2, devices)) for at in range(3)]
    same = jnp.where(up, hi[0], lo[0])
    other = [jnp.where(up, a, b) for a, b in zip(lo, hi)]
    anti = flip_matrix(False, cells_y)
    fx = (same + nn(other[0], anti, HIGHEST)) * FLUX_SCALE
    fy = jnp.sum(other[1], axis=1, keepdims=True) + reverse_rows(jnp.sum(other[2], axis=1, keepdims=True))
    fy = fy * FLUX_SCALE
    fy = [reverse_rows(fy), fy]
    side = jnp.where(up, 0, 1)
    cell = iota((cells_x, LANES), 0)
    y_wall = info[4] == 1
    for sign in range(2):
        pick = (iota((8, LANES), 0) == 1 - sign).astype(F32)
        column = tn(fx, pick, HIGHEST)
        x_wall = info[3 - sign] == 1
        ky_kind = jnp.zeros((cells_x, LANES), jnp.int32)
        for x in range(cells_x):
            ky_kind = jnp.where(cell == (x if sign else cells_x - 1 - x), kindy[side, x], ky_kind)
        fy_wide = jnp.broadcast_to(fy[sign], (cells_x, LANES))
        for at in range(per_sign):
            block = sign * per_sign + at
            ix, iy = lane_ints(first_ky, sign, at * LANES, (8, LANES))
            maxwell = jnp.exp((ix * ix + iy * iy).astype(F32) * (-UNIT * UNIT / 2.0))
            ghost = jnp.where(kx[sign] == 1.0, xw[block], column * maxwell[0:1])
            g[block, 0, 8:, :] = jnp.where(x_wall, ghost, xin(block))
            ghost_y = jnp.where(ky_kind == 1, yw[block], fy_wide * maxwell)
            value = jnp.where(y_wall, ghost_y, yin(block))
            for x in range(cells_x):
                g[block, 1 + x, 7:8, :] = value[x : x + 1]


def sweep(info, g, s, r):
    blocks, slots, padded, _ = g.shape
    cells_x, cells_y = slots - 1, padded - 8
    first_ky = info[0]

    def step(block, carry):
        ax, ay = block_speeds(first_ky, block, blocks // 2, (8, LANES))
        for x in range(cells_x - 1, -1, -1):
            for at in range(cells_y // 8 - 1, -1, -1):
                here = pl.ds(8 * at, 8)
                value = s[block, x, here, :] + ax * g[block, x, pl.ds(8 + 8 * at, 8), :]
                value += ay * g[block, 1 + x, pl.ds(7 + 8 * at, 8), :]
                value = (value * r[block, x, here, :]).astype(BF16).astype(F32)
                g[block, 1 + x, pl.ds(8 + 8 * at, 8), :] = value
        return carry

    lax.fori_loop(0, blocks, step, 0)


def send_out(info, g, xmsg, ymsg, flux):
    blocks, slots, padded, _ = g.shape
    cells_x, cells_y = slots - 1, padded - 8
    per_sign = blocks // 2
    fx = None
    for sign in range(2):
        total = jnp.zeros((cells_y, LANES), F32)
        total_y = jnp.zeros((cells_x, LANES), F32)
        for at in range(per_sign):
            block = sign * per_sign + at
            ix, iy = lane_ints(info[0], sign, at * LANES, (8, LANES))
            ix, iy = jnp.abs(ix).astype(F32), jnp.abs(iy).astype(F32)
            row = g[block, cells_x, 8:, :]
            xmsg[sign][at] = row.astype(BF16)
            total += row * ix[0:1]
            edge = jnp.concatenate([g[block, 1 + x, padded - 1 : padded, :] for x in range(cells_x)], axis=0)
            ymsg[block] = edge.astype(BF16)
            total_y += edge * iy
        pick = (iota((8, LANES), 0) == sign).astype(F32)
        part = nt(pick, total, HIGHEST)
        fx = part if fx is None else fx + part
        flux[2 - sign] = total_y
    flux[0] = fx


def first_kernel(info, kindy, ag, relax, kindx, pt, from_left, from_right, yrecv, lri, bti,
                 g, s, r, xw, yw, kx, xmsg0, xmsg1, ymsg, flux, ps):
    cells_x, _, count, cells_y = pt.shape
    per_sign = count // LANES
    blocks = 2 * per_sign
    first_ky, up = info[0], info[1] == 1
    total = [sum(ag[d, q] for d in range(ag.shape[0])) for q in range(4)]
    tau = relax[...]
    p = newton_params(total[0] * WEIGHT, total[1] * (WEIGHT * UNIT), total[2] * (WEIGHT * UNIT),
                      total[3] * (WEIGHT * UNIT * UNIT / 2.0))
    lead = p[0] - jnp.log(tau)
    rows = pieces(lead) + pieces(p[1] * UNIT) + pieces(p[2] * UNIT) + pieces(p[3] * (UNIT * UNIT / 2.0))
    rows += pieces(1.0 / TIME_STEP + 1.0 / tau)
    flip = flip_matrix(up, cells_y).astype(BF16)
    for at, piece in enumerate(rows):
        for x in range(cells_x):
            ps[x, at : at + 1, :] = piece[x : x + 1]
    for x in range(cells_x):
        ps[x, 15:16, :] = jnp.zeros((1, cells_y), F32)
    kind = jnp.concatenate([kindx[1:2], kindx[0:1], jnp.zeros((6, cells_y), jnp.int32)], axis=0).astype(F32)
    kind = nt(kind.astype(BF16), flip).astype(BF16)
    for sign in range(2):
        kx[sign] = tn(kind, (iota((8, LANES), 0) == sign).astype(F32).astype(BF16))
        for at in range(per_sign):
            block = sign * per_sign + at
            chunk = [(at * (LANES // HALF) + i) * NVX + HALF * sign for i in range(LANES // HALF)]
            part = jnp.concatenate(
                [lri[c : c + HALF, (1 - sign) * cells_y : (2 - sign) * cells_y] for c in chunk], axis=0)
            xw[block] = nt(flip, part)
            part = jnp.concatenate([bti[c : c + HALF, :] for c in chunk], axis=0)
            row, col = iota((16, cells_x), 0), iota((16, cells_x), 1)
            order = (col == (row if sign else cells_x - 1 - row)).astype(F32).astype(BF16)
            yw[block] = nt(order, part)[:cells_x]
    row = iota((16, LANES), 0)

    def build(xt, carry):
        for sign in range(2):
            x = xt if sign else cells_x - 1 - xt
            mine = nt(ps[x].astype(BF16), flip)
            table = mine.astype(BF16)
            base = tn(table, ((row >= 12) & (row < 15)).astype(F32).astype(BF16))
            for at in range(per_sign):
                block = sign * per_sign + at
                ix, iy = lane_ints(first_ky, sign, at * LANES, (16, LANES))
                energy = ix * ix + iy * iy
                basis = jnp.where(row < 3, 1, jnp.where(row < 6, ix, jnp.where(row < 9, iy, jnp.where(row < 12, energy - energy % 64, 0))))
                basis2 = jnp.where((row >= 9) & (row < 12), energy % 64, 0)
                basis = jnp.concatenate([basis, basis2], axis=0).astype(F32).astype(BF16)
                arg = tn(jnp.concatenate([table, table], axis=0), basis)
                value = nt(flip, pt[x, sign, at * LANES : (at + 1) * LANES, :])
                g[block, 1 + xt, 8:, :] = value
                s[block, xt] = value * (1.0 / TIME_STEP) + jnp.exp(arg)
                ax, ay = block_speeds(first_ky, block, per_sign, (8, LANES))
                r[block, xt] = 1.0 / (base + (ax + ay)[0:1])
        return carry

    lax.fori_loop(0, cells_x, build, 0)

    def xin(block):
        source = from_left if block >= per_sign else from_right
        at = block % per_sign
        return nt(flip, source[at * LANES : (at + 1) * LANES, :])

    def yin(block):
        at = block % per_sign
        return yrecv[block // per_sign, :, at * LANES : (at + 1) * LANES].astype(F32)

    fill_inflow(info, kindy, ag.at[:, 4:7], g, xin, yin, xw, yw, kx)
    sweep(info, g, s, r)
    send_out(info, g, (xmsg0, xmsg1), ymsg, flux)


def next_kernel(last, info, kindy, ag, from_left, from_right, yrecv, xw, yw, kx, s, r, g_in, *outs):
    blocks, slots, padded, _ = g_in.shape
    per_sign = blocks // 2
    if last:
        out, g = outs
    else:
        g, xmsg0, xmsg1, ymsg, flux = outs

    def xin(block):
        source = from_left if block >= per_sign else from_right
        return source[block % per_sign].astype(F32)

    def yin(block):
        return yrecv[block].astype(F32)

    fill_inflow(info, kindy, ag, g, xin, yin, xw, yw, kx)
    sweep(info, g, s, r)
    if not last:
        send_out(info, g, (xmsg0, xmsg1), ymsg, flux)
        return
    cells_x, cells_y = slots - 1, padded - 8
    flip = flip_matrix(info[1] == 1, cells_y).astype(BF16)

    def emit(xt, carry):
        for sign in range(2):
            x = xt if sign else cells_x - 1 - xt
            for at in range(per_sign):
                value = g[sign * per_sign + at, 1 + xt, 8:, :].astype(BF16)
                out[x, sign, at * LANES : (at + 1) * LANES, :] = tn(value, flip).astype(BF16)
        return carry

    lax.fori_loop(0, cells_x, emit, 0)


def call(kernel, outs, n_smem, ins, scratch=(), aliases=None, mib=20):
    vmem = pl.BlockSpec(memory_space=pltpu.VMEM)
    smem = pl.BlockSpec(memory_space=pltpu.SMEM)
    return pl.pallas_call(
        kernel,
        out_shape=outs,
        in_specs=[smem] * n_smem + [vmem] * (len(ins) - n_smem),
        out_specs=jax.tree.map(lambda _: vmem, outs),
        scratch_shapes=list(scratch),
        input_output_aliases=aliases or {},
        compiler_params=pltpu.CompilerParams(vmem_limit_bytes=mib << 20),
    )(*ins)


def body(previous, relax_time, left_right_kind, bottom_top_kind, left_right_inflow, bottom_top_inflow):
    vel_rows, cells_x, cells_y = previous.shape
    local_ky = vel_rows // NVX
    count = local_ky * HALF
    per_sign = count // LANES
    blocks = 2 * per_sign
    nvel, ngx, ngy = lax.axis_size("vel"), lax.axis_size("gx"), lax.axis_size("gy")
    v, ix, iy = lax.axis_index("vel"), lax.axis_index("gx"), lax.axis_index("gy")
    up = v >= nvel // 2
    y_wall = jnp.where(up, iy == 0, iy == ngy - 1)
    info = jnp.stack([v * local_ky, up.astype(jnp.int32), (ix == 0).astype(jnp.int32),
                      (ix == ngx - 1).astype(jnp.int32), y_wall.astype(jnp.int32)])
    right = [(i, i + 1) for i in range(ngx - 1)]
    left = [(i + 1, i) for i in range(ngx - 1)]
    along = []
    for d in range(nvel):
        for j in range(ngy - 1):
            along.append((d * ngy + j, d * ngy + j + 1) if d >= nvel // 2 else (d * ngy + j + 1, d * ngy + j))

    def shift_y(a):
        return lax.ppermute(a, ("vel", "gy"), along)

    pt = previous.reshape(local_ky, 2, HALF, cells_x, cells_y).transpose(3, 1, 0, 2, 4)
    pt = pt.reshape(cells_x, 2, count, cells_y)
    from_left = lax.ppermute(pt[cells_x - 1, 1], "gx", right)
    from_right = lax.ppermute(pt[0, 0], "gx", left)
    sds = jax.ShapeDtypeStruct
    pay, ymsg = call(
        moments_kernel,
        (sds((7, 8, LANES), F32), sds((2, cells_x, count), BF16)),
        1, (info, pt), mib=16)
    yrecv = shift_y(ymsg)
    ag = lax.all_gather(pay, "vel")
    lri = left_right_inflow.reshape(vel_rows, 2 * cells_y)
    bti = jnp.where(up, bottom_top_inflow[:, 0, :], bottom_top_inflow[:, 1, :])
    g_shape = sds((blocks, cells_x + 1, cells_y + 8, LANES), F32)
    full = sds((blocks, cells_x, cells_y, LANES), F32)
    messages = (sds((per_sign, cells_y, LANES), BF16), sds((per_sign, cells_y, LANES), BF16),
                sds((blocks, cells_x, LANES), BF16), sds((3, 8, LANES), F32))
    g, s, r, xw, yw, kx, xmsg0, xmsg1, ymsg, flux = call(
        first_kernel,
        (g_shape, full, full, sds((blocks, cells_y, LANES), F32), sds((blocks, cells_x, LANES), F32),
         sds((2, cells_y, LANES), F32)) + messages,
        2,
        (info, bottom_top_kind, ag, relax_time, left_right_kind, pt, from_left, from_right, yrecv, lri, bti),
        scratch=[pltpu.VMEM((cells_x, 16, cells_y), F32)], mib=32)
    for number in range(1, SWEEPS):
        from_left = lax.ppermute(xmsg1, "gx", right)
        from_right = lax.ppermute(xmsg0, "gx", left)
        yrecv = shift_y(ymsg)
        ag = lax.all_gather(flux, "vel")
        last = number == SWEEPS - 1
        ins = (info, bottom_top_kind, ag, from_left, from_right, yrecv, xw, yw, kx, s, r, g)
        if last:
            out, _ = call(functools.partial(next_kernel, True),
                          (sds((cells_x, 2, count, cells_y), BF16), g_shape), 2, ins, aliases={11: 1}, mib=32)
        else:
            g, xmsg0, xmsg1, ymsg, flux = call(
                functools.partial(next_kernel, False), (g_shape,) + messages, 2, ins, aliases={11: 0}, mib=32)
    out = out.reshape(cells_x, 2, local_ky, HALF, cells_y).transpose(2, 1, 3, 0, 4)
    return out.reshape(vel_rows, cells_x, cells_y)


def solution(mesh):
    return jax.shard_map(
        body,
        mesh=mesh,
        in_specs=(P("vel", "gx", "gy"), P("gx", "gy"), P(None, "gy"), P(None, "gx"), P("vel", None, "gy"), P("vel", None, "gx")),
        out_specs=P("vel", "gx", "gy"),
        check_vma=False,
    )
```

```python
import functools
import math

import jax
import jax.numpy as jnp
import numpy as np
from jax import lax
from jax.experimental import pallas as pl
from jax.experimental.pallas import tpu as pltpu
from jax.sharding import PartitionSpec as P

NVX = 64
HALF = NVX // 2
NEWTON = 2
SWEEPS = 4
COURANT = 100.0
STEP = 12.0 / NVX
UNIT = STEP / 2.0
WEIGHT = STEP * STEP / (2.0 * math.pi)
TIME_STEP = COURANT / ((NVX - 1) * STEP)
LANES = 128
HIGHEST = lax.Precision.HIGHEST
F32 = jnp.float32
BF16 = jnp.bfloat16


def wall_norm_value():
    line = (np.arange(NVX) - (NVX - 1) / 2.0) * STEP
    gauss = np.exp(-line * line / 2.0)
    return float(np.sum(np.maximum(line, 0.0) * gauss) * np.sum(gauss) * WEIGHT)


FLUX_SCALE = WEIGHT * UNIT / wall_norm_value()


def nn(a, b, precision=None):
    return lax.dot_general(a, b, (((1,), (0,)), ((), ())), precision=precision, preferred_element_type=F32)


def nt(a, b, precision=None):
    return lax.dot_general(a, b, (((1,), (1,)), ((), ())), precision=precision, preferred_element_type=F32)


def tn(a, b, precision=None):
    return lax.dot_general(a, b, (((0,), (0,)), ((), ())), precision=precision, preferred_element_type=F32)


def iota(shape, dim):
    return lax.broadcasted_iota(jnp.int32, shape, dim)


def lane_ints(first_ky, sign, start, shape):
    lane = iota(shape, len(shape) - 1) + start
    ix = 2 * (lane % HALF + HALF * sign) - (NVX - 1)
    iy = 2 * (first_ky + lane // HALF) - (NVX - 1)
    return ix, iy


def flip_matrix(up, size):
    row, col = iota((size, size), 0), iota((size, size), 1)
    return (col == jnp.where(up, row, size - 1 - row)).astype(F32)


def reverse_rows(a):
    return jnp.concatenate([a[i : i + 1] for i in range(a.shape[0] - 1, -1, -1)], axis=0)


def pieces(a):
    high = a.astype(BF16).astype(F32)
    rest = a - high
    middle = rest.astype(BF16).astype(F32)
    return [high, middle, rest - middle]


def moments_kernel(info, prev, pay, ymsg, pt, xmsg0, xmsg1, rows):
    cells_x, _, count, cells_y = pt.shape
    span = HALF * cells_x
    for sign in range(2):
        for at in range(count // LANES):
            for i in range(LANES // HALF):
                start = ((at * (LANES // HALF) + i) * NVX + sign * HALF) * cells_x
                rows[i * span : (i + 1) * span, :] = prev[start : start + span, :].astype(F32)
            for x in range(cells_x):
                pt[x, sign, at * LANES : (at + 1) * LANES, :] = rows[pl.ds(x, LANES, stride=cells_x), :].astype(BF16)
    even = info[5]
    xmsg0[...] = pt[(cells_x - 1) * even, even]
    xmsg1[...] = pt[(cells_x - 1) * (1 - even), 1 - even]
    first_ky, up = info[0], info[1] == 1
    y_out = jnp.where(up, cells_y - 1, 0)
    row = iota((16, count), 0)
    weights = []
    for sign in range(2):
        ix, iy = lane_ints(first_ky, sign, 0, (16, count))
        energy = ix * ix + iy * iy
        low = energy % 64
        table = jnp.where(row == 0, 1, jnp.where(row == 1, ix, jnp.where(row == 2, iy, jnp.where(
            row == 3, energy - low, jnp.where(row == 4, low, jnp.where(row == 5, jnp.abs(ix), 0))))))
        weights.append(table.astype(F32).astype(BF16))
    edge = [jnp.zeros((16, count), F32) for _ in range(2)]
    out_row = [None, None]
    pick_row, pick_col = iota((16, cells_y), 0), iota((16, cells_y), 1)
    for x in range(cells_x):
        total = None
        for sign in range(2):
            block = pt[x, sign]
            part = nn(weights[sign], block)
            if x == (cells_x - 1) * sign:
                out_row[sign] = part[5:6]
            total = part if total is None else total + part
            at = x if sign else cells_x - 1 - x
            pick = ((pick_row == at) & (pick_col == y_out)).astype(F32).astype(BF16)
            edge[sign] = edge[sign] + nt(pick, block)
        pay[0, x : x + 1, :] = total[0:1]
        pay[1, x : x + 1, :] = total[1:2]
        pay[2, x : x + 1, :] = total[2:3]
        pay[3, x : x + 1, :] = total[3:4] + total[4:5]
    flip = flip_matrix(up, cells_y)
    fx = jnp.concatenate([out_row[0], out_row[1], jnp.zeros((6, cells_y), F32)], axis=0)
    pay[4] = nt(fx, flip, HIGHEST)
    for sign in range(2):
        total = jnp.zeros((cells_x, LANES), F32)
        for at in range(count // LANES):
            _, iy = lane_ints(first_ky, sign, at * LANES, (cells_x, LANES))
            total += jnp.abs(iy).astype(F32) * edge[sign][:cells_x, at * LANES : (at + 1) * LANES]
        pay[6 - sign] = total
        ymsg[sign] = edge[sign][:cells_x].astype(BF16)


def newton_params(u0, u1, u2, u3):
    ux, uy = u1 / u0, u2 / u0
    square = ux * ux + uy * uy
    temperature = u3 / u0 - square / 2.0
    p = [jnp.log(u0 / temperature) - square / (2.0 * temperature), ux / temperature, uy / temperature, -1.0 / temperature]
    line = [float((i - (NVX - 1) / 2.0) * STEP) for i in range(NVX)]
    for _ in range(NEWTON):
        half_p3 = p[3] * 0.5
        sums, tops = [], []
        for slope in (p[1], p[2]):
            top = None
            for value in line:
                arg = value * (slope + value * half_p3)
                top = arg if top is None else jnp.maximum(top, arg)
            total = [None] * 5
            for value in line:
                term = jnp.exp(value * (slope + value * half_p3) - top)
                for power in range(5):
                    total[power] = term if total[power] is None else total[power] + term
                    term = term * value
            sums.append(total)
            tops.append(top)
        scale = jnp.exp(p[0] + (tops[0] + tops[1])) * WEIGHT
        x = sums[0]
        y = [scale * t for t in sums[1]]
        x2, y2 = x[2] * y[0], x[0] * y[2]
        n = [x[0] * y[0], x[1] * y[0], x[0] * y[1], (x2 + y2) * 0.5, x2, x[1] * y[1],
             (x[3] * y[0] + x[1] * y[2]) * 0.5, y2, (x[2] * y[1] + x[0] * y[3]) * 0.5,
             (x[4] * y[0] + 2.0 * (x[2] * y[2]) + x[0] * y[4]) * 0.25]
        layout = [[0, 1, 2, 3], [1, 4, 5, 6], [2, 5, 7, 8], [3, 6, 8, 9]]
        matrix = [[n[layout[r][c]] for c in range(4)] for r in range(4)]
        target = [n[0] - u0, n[1] - u1, n[2] - u2, n[3] - u3]
        for pivot in range(4):
            for lower in range(pivot + 1, 4):
                factor = matrix[lower][pivot] / matrix[pivot][pivot]
                for col in range(pivot, 4):
                    matrix[lower][col] = matrix[lower][col] - factor * matrix[pivot][col]
                target[lower] = target[lower] - factor * target[pivot]
        result = [None] * 4
        for pivot in (3, 2, 1, 0):
            accum = target[pivot]
            for col in range(pivot + 1, 4):
                accum = accum - matrix[pivot][col] * result[col]
            result[pivot] = accum / matrix[pivot][pivot]
        p = [a - b for a, b in zip(p, result)]
    return p


def block_speeds(first_ky, block, per_sign, shape):
    ix, iy = lane_ints(first_ky, block // per_sign, (block % per_sign) * LANES, shape)
    return jnp.abs(ix).astype(F32) * UNIT, jnp.abs(iy).astype(F32) * UNIT


def fill_inflow(info, kindy, same, other, g, xin, yin, xw, yw, kx):
    blocks, slots, padded, _ = g.shape
    cells_x, cells_y = slots - 1, padded - 8
    per_sign = blocks // 2
    first_ky, up = info[0], info[1] == 1
    anti = flip_matrix(False, cells_y)
    fx = (same[0] + nn(other[0], anti, HIGHEST)) * FLUX_SCALE
    fy = jnp.sum(other[1], axis=1, keepdims=True) + reverse_rows(jnp.sum(other[2], axis=1, keepdims=True))
    fy = fy * FLUX_SCALE
    fy = [reverse_rows(fy), fy]
    side = jnp.where(up, 0, 1)
    cell = iota((cells_x, LANES), 0)
    y_wall = info[4] == 1
    for sign in range(2):
        pick = (iota((8, LANES), 0) == 1 - sign).astype(F32)
        column = tn(fx, pick, HIGHEST)
        x_wall = info[3 - sign] == 1
        ky_kind = jnp.zeros((cells_x, LANES), jnp.int32)
        for x in range(cells_x):
            ky_kind = jnp.where(cell == (x if sign else cells_x - 1 - x), kindy[side, x], ky_kind)
        fy_wide = jnp.broadcast_to(fy[sign], (cells_x, LANES))
        for at in range(per_sign):
            block = sign * per_sign + at
            ix, iy = lane_ints(first_ky, sign, at * LANES, (8, LANES))
            maxwell = jnp.exp((ix * ix + iy * iy).astype(F32) * (-UNIT * UNIT / 2.0))
            ghost = jnp.where(kx[sign] == 1.0, xw[block], column * maxwell[0:1])
            g[block, 0, 8:, :] = jnp.where(x_wall, ghost, xin(block))
            ghost_y = jnp.where(ky_kind == 1, yw[block], fy_wide * maxwell)
            value = jnp.where(y_wall, ghost_y, yin(block))
            for x in range(cells_x):
                g[block, 1 + x, 7:8, :] = value[x : x + 1]


def sweep(info, g, s, r):
    blocks, slots, padded, _ = g.shape
    cells_x, cells_y = slots - 1, padded - 8
    first_ky = info[0]

    def step(block, carry):
        ax, ay = block_speeds(first_ky, block, blocks // 2, (8, LANES))
        for x in range(cells_x - 1, -1, -1):
            for at in range(cells_y // 8 - 1, -1, -1):
                here = pl.ds(8 * at, 8)
                value = s[block, x, here, :] + ax * g[block, x, pl.ds(8 + 8 * at, 8), :]
                value += ay * g[block, 1 + x, pl.ds(7 + 8 * at, 8), :]
                value = (value * r[block, x, here, :]).astype(BF16).astype(F32)
                g[block, 1 + x, pl.ds(8 + 8 * at, 8), :] = value
        return carry

    lax.fori_loop(0, blocks, step, 0)


def send_out(info, g, xmsg, ymsg, flux):
    blocks, slots, padded, _ = g.shape
    cells_x, cells_y = slots - 1, padded - 8
    per_sign = blocks // 2
    fx = None
    for sign in range(2):
        total = jnp.zeros((cells_y, LANES), F32)
        total_y = jnp.zeros((cells_x, LANES), F32)
        for at in range(per_sign):
            block = sign * per_sign + at
            ix, iy = lane_ints(info[0], sign, at * LANES, (8, LANES))
            ix, iy = jnp.abs(ix).astype(F32), jnp.abs(iy).astype(F32)
            row = g[block, cells_x, 8:, :]
            total += row * ix[0:1]
            edge = jnp.concatenate([g[block, 1 + x, padded - 1 : padded, :] for x in range(cells_x)], axis=0)
            ymsg[block] = edge.astype(BF16)
            total_y += edge * iy
        for at in range(per_sign):
            take = sign * (1 - info[5]) + (1 - sign) * info[5]
            xmsg[sign][at] = g[take * per_sign + at, cells_x, 8:, :].astype(BF16)
        pick = (iota((8, LANES), 0) == sign).astype(F32)
        part = nt(pick, total, HIGHEST)
        fx = part if fx is None else fx + part
        flux[2 - sign] = total_y
    flux[0] = fx


def first_kernel(info, kindy, same, other, relax, kindx, pt, pair0, pair1, yrecv, lri, bti,
                 g, s, r, xw, yw, kx, xmsg0, xmsg1, ymsg, flux, ta, tb, tr, fa, fb):
    cells_x, _, count, cells_y = pt.shape
    per_sign = count // LANES
    blocks = 2 * per_sign
    first_ky, up = info[0], info[1] == 1
    total = [same[q] + other[q] for q in range(4)]
    tau = relax[...]
    p = newton_params(total[0] * WEIGHT, total[1] * (WEIGHT * UNIT), total[2] * (WEIGHT * UNIT),
                      total[3] * (WEIGHT * UNIT * UNIT / 2.0))
    lead = p[0] - jnp.log(tau)
    flip = flip_matrix(up, cells_y).astype(BF16)
    local_ky = count // HALF
    vx = (2 * iota((NVX, cells_y), 0) - (NVX - 1)).astype(F32) * UNIT
    vy = (2 * (first_ky + iota((local_ky, cells_y), 0)) - (NVX - 1)).astype(F32) * UNIT
    steps = iota((NVX, cells_y), 0).astype(F32) * STEP
    half_p3 = p[3] * 0.5
    base = 1.0 / TIME_STEP + 1.0 / tau
    for x in range(cells_x):
        here = slice(x, x + 1)
        arg = vy * (p[2][here] + vy * half_p3[here])
        top = jnp.max(arg, axis=0, keepdims=True)
        along_y = jnp.exp(arg - top)
        along_x = jnp.exp((lead[here] + top) + vx * (p[1][here] + vx * half_p3[here]))
        inverse = 1.0 / (base[here] + steps)
        for table, ref in ((along_x, ta), (along_y, tb), (inverse, tr)):
            wide = nt(flip, jnp.concatenate(pieces(table), axis=0).astype(BF16)).astype(BF16)
            ref[1, x * cells_y : (x + 1) * cells_y, :] = wide
            ref[0, (cells_x - 1 - x) * cells_y : (cells_x - x) * cells_y, :] = wide
    kind = jnp.concatenate([kindx[1:2], kindx[0:1], jnp.zeros((6, cells_y), jnp.int32)], axis=0).astype(F32)
    kind = nt(kind.astype(BF16), flip).astype(BF16)
    for sign in range(2):
        kx[sign] = tn(kind, (iota((8, LANES), 0) == sign).astype(F32).astype(BF16))
        for at in range(per_sign):
            block = sign * per_sign + at
            chunk = [(at * (LANES // HALF) + i) * NVX + HALF * sign for i in range(LANES // HALF)]
            part = jnp.concatenate(
                [lri[c : c + HALF, (1 - sign) * cells_y : (2 - sign) * cells_y] for c in chunk], axis=0)
            xw[block] = nt(flip, part)
            part = jnp.concatenate([bti[c : c + HALF, :] for c in chunk], axis=0)
            row, col = iota((16, cells_x), 0), iota((16, cells_x), 1)
            order = (col == (row if sign else cells_x - 1 - row)).astype(F32).astype(BF16)
            yw[block] = nt(order, part)[:cells_x]
    def spread(ref, sign, choice, size):
        row = iota((3 * size, LANES), 0) % size
        return nn(ref[sign], (row == choice).astype(F32).astype(BF16))

    for sign in range(2):
        fa[...] = spread(ta, sign, iota((1, LANES), 1) % HALF + HALF * sign, NVX)
        for at in range(per_sign):
            block = sign * per_sign + at
            ix, iy = lane_ints(first_ky, sign, at * LANES, (1, LANES))
            r[block] = spread(tr, sign, (jnp.abs(ix) + jnp.abs(iy)) // 2, NVX).reshape(cells_x, cells_y, LANES)
            fb[...] = spread(tb, sign, iota((1, LANES), 1) // HALF + at * (LANES // HALF), local_ky)
            for xt in range(cells_x):
                x = xt if sign else cells_x - 1 - xt
                here = slice(xt * cells_y, (xt + 1) * cells_y)
                value = nt(flip, pt[x, sign, at * LANES : (at + 1) * LANES, :])
                g[block, 1 + xt, 8:, :] = value
                s[block, xt] = value * (1.0 / TIME_STEP) + fa[here, :] * fb[here, :]

    def xin(block):
        at = block % per_sign
        first = (info[5] == 1) == (block < per_sign)
        here = slice(at * LANES, (at + 1) * LANES)
        return nt(flip, jnp.where(first, pair0[here, :], pair1[here, :]))

    def yin(block):
        at = block % per_sign
        return yrecv[block // per_sign, :, at * LANES : (at + 1) * LANES].astype(F32)

    fill_inflow(info, kindy, same.at[4:7], other.at[4:7], g, xin, yin, xw, yw, kx)
    sweep(info, g, s, r)
    send_out(info, g, (xmsg0, xmsg1), ymsg, flux)


def next_kernel(last, info, kindy, same, other, pair0, pair1, yrecv, xw, yw, kx, s, r, g_in, *outs):
    blocks, slots, padded, _ = g_in.shape
    per_sign = blocks // 2
    if last:
        out, g, rows = outs
    else:
        g, xmsg0, xmsg1, ymsg, flux = outs

    def xin(block):
        first = (info[5] == 1) == (block < per_sign)
        return jnp.where(first, pair0[block % per_sign].astype(F32), pair1[block % per_sign].astype(F32))

    def yin(block):
        return yrecv[block].astype(F32)

    fill_inflow(info, kindy, same, other, g, xin, yin, xw, yw, kx)
    sweep(info, g, s, r)
    if not last:
        send_out(info, g, (xmsg0, xmsg1), ymsg, flux)
        return
    cells_x, cells_y = slots - 1, padded - 8
    flip = flip_matrix(info[1] == 1, cells_y).astype(BF16)

    span = HALF * cells_x
    for sign in range(2):
        for at in range(per_sign):
            for x in range(cells_x):
                xt = x if sign else cells_x - 1 - x
                value = g[sign * per_sign + at, 1 + xt, 8:, :].astype(BF16)
                rows[pl.ds(x, LANES, stride=cells_x), :] = tn(value, flip)
            for i in range(LANES // HALF):
                start = ((at * (LANES // HALF) + i) * NVX + sign * HALF) * cells_x
                out[start : start + span, :] = rows[i * span : (i + 1) * span, :].astype(BF16)


def call(kernel, outs, n_smem, ins, scratch=(), aliases=None, mib=20):
    vmem = pl.BlockSpec(memory_space=pltpu.VMEM)
    smem = pl.BlockSpec(memory_space=pltpu.SMEM)
    return pl.pallas_call(
        kernel,
        out_shape=outs,
        in_specs=[smem] * n_smem + [vmem] * (len(ins) - n_smem),
        out_specs=jax.tree.map(lambda _: vmem, outs),
        scratch_shapes=list(scratch),
        input_output_aliases=aliases or {},
        compiler_params=pltpu.CompilerParams(vmem_limit_bytes=mib << 20),
    )(*ins)


def body(previous, relax_time, left_right_kind, bottom_top_kind, left_right_inflow, bottom_top_inflow):
    vel_rows, cells_x, cells_y = previous.shape
    local_ky = vel_rows // NVX
    count = local_ky * HALF
    per_sign = count // LANES
    blocks = 2 * per_sign
    nvel, ngx, ngy = lax.axis_size("vel"), lax.axis_size("gx"), lax.axis_size("gy")
    v, ix, iy = lax.axis_index("vel"), lax.axis_index("gx"), lax.axis_index("gy")
    up = v >= nvel // 2
    y_wall = jnp.where(up, iy == 0, iy == ngy - 1)
    info = jnp.stack([v * local_ky, up.astype(jnp.int32), (ix == 0).astype(jnp.int32),
                      (ix == ngx - 1).astype(jnp.int32), y_wall.astype(jnp.int32), (ix % 2 == 0).astype(jnp.int32)])
    def pairs(count, start):
        low = range(start, count - 1, 2)
        return [(i, i + 1) for i in low] + [(i + 1, i) for i in low]

    def swap_x(first, second):
        return lax.ppermute(first, "gx", pairs(ngx, 0)), lax.ppermute(second, "gx", pairs(ngx, 1))

    def swap_y(a):
        return lax.ppermute(a, "gy", pairs(ngy, 0))

    def sum_vel(a):
        reach = 1
        while reach < nvel // 2:
            a = a + lax.ppermute(a, "vel", [(i, i ^ reach) for i in range(nvel)])
            reach *= 2
        return a, lax.ppermute(a, "vel", [(i, i ^ reach) for i in range(nvel)])

    assert ngy == 2 and nvel & (nvel - 1) == 0, "mesh shape"
    sds = jax.ShapeDtypeStruct
    pay, ymsg, pt, xmsg0, xmsg1 = call(
        moments_kernel,
        (sds((7, 8, LANES), F32), sds((2, cells_x, count), BF16), sds((cells_x, 2, count, cells_y), BF16),
         sds((count, cells_y), BF16), sds((count, cells_y), BF16)),
        1, (info, previous.reshape(vel_rows * cells_x, cells_y)),
        scratch=[pltpu.VMEM((LANES * cells_x, cells_y), F32)], mib=8)
    halo = swap_x(xmsg0, xmsg1)
    yrecv = swap_y(ymsg)
    sums = sum_vel(pay)
    lri = left_right_inflow.reshape(vel_rows, 2 * cells_y)
    bti = jnp.where(up, bottom_top_inflow[:, 0, :], bottom_top_inflow[:, 1, :])
    g_shape = sds((blocks, cells_x + 1, cells_y + 8, LANES), F32)
    full = sds((blocks, cells_x, cells_y, LANES), F32)
    messages = (sds((per_sign, cells_y, LANES), BF16), sds((per_sign, cells_y, LANES), BF16),
                sds((blocks, cells_x, LANES), BF16), sds((3, 8, LANES), F32))
    g, s, r, xw, yw, kx, xmsg0, xmsg1, ymsg, flux = call(
        first_kernel,
        (g_shape, full, full, sds((blocks, cells_y, LANES), F32), sds((blocks, cells_x, LANES), F32),
         sds((2, cells_y, LANES), F32)) + messages,
        2,
        (info, bottom_top_kind, *sums, relax_time, left_right_kind, pt, *halo, yrecv, lri, bti),
        scratch=[
            pltpu.VMEM((2, cells_x * cells_y, 3 * NVX), BF16), pltpu.VMEM((2, cells_x * cells_y, 3 * local_ky), BF16),
            pltpu.VMEM((2, cells_x * cells_y, 3 * NVX), BF16), pltpu.VMEM((cells_x * cells_y, LANES), F32),
            pltpu.VMEM((cells_x * cells_y, LANES), F32)], mib=24)
    for number in range(1, SWEEPS):
        halo = swap_x(xmsg0, xmsg1)
        yrecv = swap_y(ymsg)
        sums = sum_vel(flux)
        last = number == SWEEPS - 1
        ins = (info, bottom_top_kind, *sums, *halo, yrecv, xw, yw, kx, s, r, g)
        if last:
            out, _ = call(functools.partial(next_kernel, True),
                          (sds((vel_rows * cells_x, cells_y), BF16), g_shape), 2, ins, aliases={12: 1},
                          scratch=[pltpu.VMEM((LANES * cells_x, cells_y), F32)], mib=22)
        else:
            g, xmsg0, xmsg1, ymsg, flux = call(
                functools.partial(next_kernel, False), (g_shape,) + messages, 2, ins, aliases={12: 0}, mib=22)
    return out.reshape(vel_rows, cells_x, cells_y)


def solution(mesh):
    return jax.shard_map(
        body,
        mesh=mesh,
        in_specs=(P("vel", "gx", "gy"), P("gx", "gy"), P(None, "gy"), P(None, "gx"), P("vel", None, "gy"), P("vel", None, "gx")),
        out_specs=P("vel", "gx", "gy"),
        check_vma=False,
    )
```

```python
import functools
import math

import jax
import jax.numpy as jnp
import numpy as np
from jax import lax
from jax.experimental import pallas as pl
from jax.experimental.pallas import tpu as pltpu
from jax.sharding import PartitionSpec as P

NVX = 64
HALF = NVX // 2
NEWTON = 2
SWEEPS = 4
COURANT = 100.0
STEP = 12.0 / NVX
UNIT = STEP / 2.0
WEIGHT = STEP * STEP / (2.0 * math.pi)
TIME_STEP = COURANT / ((NVX - 1) * STEP)
LANES = 128
HIGHEST = lax.Precision.HIGHEST
F32 = jnp.float32
BF16 = jnp.bfloat16


def wall_norm_value():
    line = (np.arange(NVX) - (NVX - 1) / 2.0) * STEP
    gauss = np.exp(-line * line / 2.0)
    return float(np.sum(np.maximum(line, 0.0) * gauss) * np.sum(gauss) * WEIGHT)


FLUX_SCALE = WEIGHT * UNIT / wall_norm_value()


def nn(a, b, precision=None):
    return lax.dot_general(a, b, (((1,), (0,)), ((), ())), precision=precision, preferred_element_type=F32)


def nt(a, b, precision=None):
    return lax.dot_general(a, b, (((1,), (1,)), ((), ())), precision=precision, preferred_element_type=F32)


def tn(a, b, precision=None):
    return lax.dot_general(a, b, (((0,), (0,)), ((), ())), precision=precision, preferred_element_type=F32)


def iota(shape, dim):
    return lax.broadcasted_iota(jnp.int32, shape, dim)


def lane_ints(first_ky, sign, start, shape):
    lane = iota(shape, len(shape) - 1) + start
    ix = 2 * (lane % HALF + HALF * sign) - (NVX - 1)
    iy = 2 * (first_ky + lane // HALF) - (NVX - 1)
    return ix, iy


def device_info(local_ky):
    v, ix, iy = lax.axis_index("vel"), lax.axis_index("gx"), lax.axis_index("gy")
    up = (v >= lax.axis_size("vel") // 2).astype(jnp.int32)
    wall = jnp.where(iy == jnp.where(up == 1, 0, lax.axis_size("gy") - 1), 1, 0)
    first, last = (ix == 0).astype(jnp.int32), (ix == lax.axis_size("gx") - 1).astype(jnp.int32)
    return [v * local_ky, up, first, last, wall, 1 - lax.rem(ix, 2)]


def flip_matrix(up, size):
    row, col = iota((size, size), 0), iota((size, size), 1)
    return (col == jnp.where(up, row, size - 1 - row)).astype(F32)


def reverse_rows(a):
    return jnp.concatenate([a[i : i + 1] for i in range(a.shape[0] - 1, -1, -1)], axis=0)


def pieces(a):
    high = a.astype(BF16).astype(F32)
    rest = a - high
    middle = rest.astype(BF16).astype(F32)
    return [high, middle, rest - middle]


def stacked(a):
    return jnp.concatenate(pieces(a), axis=0).astype(BF16)


def moments_kernel(prev, relax_far, kindx_far, pay, ymsg, pt, xmsg0, xmsg1, relax, kindx, rows, staged, sems, few):
    cells_x, _, count, cells_y = pt.shape
    info = device_info(count // HALF)
    span = HALF * cells_x
    copies = [pltpu.make_async_copy(prev.at[pl.ds(i * span, span), :], staged.at[pl.ds(i * span, span), :], sems.at[i])
              for i in range(2 * count // HALF)]
    order = [2 * i + sign for sign in range(2) for i in range(count // HALF)]
    for i in order:
        copies[i].start()
    small = [pltpu.make_async_copy(relax_far, relax, few.at[0]), pltpu.make_async_copy(kindx_far, kindx, few.at[1])]
    for copy in small:
        copy.start()
    for sign in range(2):
        for at in range(count // LANES):
            for i in range(LANES // HALF):
                chunk = (at * (LANES // HALF) + i) * 2 + sign
                copies[chunk].wait()
                rows[i * span : (i + 1) * span, :] = staged[chunk * span : (chunk + 1) * span, :].astype(F32)
            for x in range(cells_x):
                pt[x, sign, at * LANES : (at + 1) * LANES, :] = rows[pl.ds(x, LANES, stride=cells_x), :].astype(BF16)
    even = info[5]
    xmsg0[...] = pt[(cells_x - 1) * even, even]
    xmsg1[...] = pt[(cells_x - 1) * (1 - even), 1 - even]
    first_ky, up = info[0], info[1] == 1
    y_out = jnp.where(up, cells_y - 1, 0)
    row = iota((16, count), 0)
    weights = []
    for sign in range(2):
        ix, iy = lane_ints(first_ky, sign, 0, (16, count))
        energy = ix * ix + iy * iy
        low = energy % 64
        table = jnp.where(row == 0, 1, jnp.where(row == 1, ix, jnp.where(row == 2, iy, jnp.where(
            row == 3, energy - low, jnp.where(row == 4, low, jnp.where(row == 5, jnp.abs(ix), 0))))))
        weights.append(table.astype(F32).astype(BF16))
    edge = [jnp.zeros((16, count), F32) for _ in range(2)]
    out_row = [None, None]
    pick_row, pick_col = iota((16, cells_y), 0), iota((16, cells_y), 1)
    for x in range(cells_x):
        total = None
        for sign in range(2):
            block = pt[x, sign]
            part = nn(weights[sign], block)
            if x == (cells_x - 1) * sign:
                out_row[sign] = part[5:6]
            total = part if total is None else total + part
            at = x if sign else cells_x - 1 - x
            pick = ((pick_row == at) & (pick_col == y_out)).astype(F32).astype(BF16)
            edge[sign] = edge[sign] + nt(pick, block)
        pay[0, x : x + 1, :] = total[0:1]
        pay[1, x : x + 1, :] = total[1:2]
        pay[2, x : x + 1, :] = total[2:3]
        pay[3, x : x + 1, :] = total[3:4] + total[4:5]
    flip = flip_matrix(up, cells_y)
    fx = jnp.concatenate([out_row[0], out_row[1], jnp.zeros((6, cells_y), F32)], axis=0)
    turned = nt(stacked(fx), flip.astype(BF16))
    pay[4] = turned[0:8] + turned[8:16] + turned[16:24]
    for sign in range(2):
        total = jnp.zeros((cells_x, LANES), F32)
        for at in range(count // LANES):
            _, iy = lane_ints(first_ky, sign, at * LANES, (cells_x, LANES))
            total += jnp.abs(iy).astype(F32) * edge[sign][:cells_x, at * LANES : (at + 1) * LANES]
        pay[6 - sign] = total
        ymsg[sign] = edge[sign][:cells_x].astype(BF16)
    for copy in small:
        copy.wait()


def newton_params(u0, u1, u2, u3):
    ux, uy = u1 / u0, u2 / u0
    square = ux * ux + uy * uy
    temperature = u3 / u0 - square / 2.0
    p = [jnp.log(u0 / temperature) - square / (2.0 * temperature), ux / temperature, uy / temperature, -1.0 / temperature]
    last = (HALF - 0.5) * STEP
    for _ in range(NEWTON):
        half_p3 = p[3] * 0.5
        sums, tops = [], []
        for slope in (p[1], p[2]):
            vertex = jnp.where(p[3] < 0.0, -slope / p[3], 0.0) * (1.0 / STEP)
            node = (jnp.clip(jnp.floor(vertex), -HALF, HALF - 1.0) + 0.5) * STEP
            end = (last * last) * half_p3 + last * jnp.abs(slope)
            top = jnp.maximum(node * (slope + node * half_p3), end)
            total = [None] * 5
            for i in range(HALF):
                value = (i + 0.5) * STEP
                even, odd = (value * value) * half_p3 - top, value * slope
                plus, minus = jnp.exp(even + odd), jnp.exp(even - odd)
                even, odd = plus + minus, plus - minus
                terms = [even, value * odd, value**2 * even, value**3 * odd, value**4 * even]
                total = [t if old is None else old + t for old, t in zip(total, terms)]
            sums.append(total)
            tops.append(top)
        scale = jnp.exp(p[0] + (tops[0] + tops[1])) * WEIGHT
        x = sums[0]
        y = [scale * t for t in sums[1]]
        x2, y2 = x[2] * y[0], x[0] * y[2]
        n = [x[0] * y[0], x[1] * y[0], x[0] * y[1], (x2 + y2) * 0.5, x2, x[1] * y[1],
             (x[3] * y[0] + x[1] * y[2]) * 0.5, y2, (x[2] * y[1] + x[0] * y[3]) * 0.5,
             (x[4] * y[0] + 2.0 * (x[2] * y[2]) + x[0] * y[4]) * 0.25]
        layout = [[0, 1, 2, 3], [1, 4, 5, 6], [2, 5, 7, 8], [3, 6, 8, 9]]
        matrix = [[n[layout[r][c]] for c in range(4)] for r in range(4)]
        target = [n[0] - u0, n[1] - u1, n[2] - u2, n[3] - u3]
        for pivot in range(4):
            for lower in range(pivot + 1, 4):
                factor = matrix[lower][pivot] / matrix[pivot][pivot]
                for col in range(pivot, 4):
                    matrix[lower][col] = matrix[lower][col] - factor * matrix[pivot][col]
                target[lower] = target[lower] - factor * target[pivot]
        result = [None] * 4
        for pivot in (3, 2, 1, 0):
            accum = target[pivot]
            for col in range(pivot + 1, 4):
                accum = accum - matrix[pivot][col] * result[col]
            result[pivot] = accum / matrix[pivot][pivot]
        p = [a - b for a, b in zip(p, result)]
    return p


def block_speeds(first_ky, block, per_sign, shape):
    ix, iy = lane_ints(first_ky, block // per_sign, (block % per_sign) * LANES, shape)
    return jnp.abs(ix).astype(F32) * UNIT, jnp.abs(iy).astype(F32) * UNIT


def fill_inflow(info, kindy, same, other, g, xin, yin, xw, yw, kx):
    blocks, slots, padded, _ = g.shape
    cells_x, cells_y = slots - 1, padded - 8
    per_sign = blocks // 2
    first_ky, up = info[0], info[1] == 1
    anti = flip_matrix(False, cells_y)
    turned = nn(stacked(other[0]), anti.astype(BF16))
    fx = (same[0] + (turned[0:8] + turned[8:16] + turned[16:24])) * FLUX_SCALE
    lane = iota((24, 2 * LANES), 1) // LANES
    columns = tn(stacked(fx), (iota((24, 2 * LANES), 0) % 8 == 1 - lane).astype(F32).astype(BF16))
    fy = jnp.sum(other[1], axis=1, keepdims=True) + reverse_rows(jnp.sum(other[2], axis=1, keepdims=True))
    fy = fy * FLUX_SCALE
    fy = [reverse_rows(fy), fy]
    side = jnp.where(up, 0, 1)
    cell = iota((cells_x, LANES), 0)
    y_wall = info[4] == 1
    for sign in range(2):
        column = columns[:, sign * LANES : (sign + 1) * LANES]
        x_wall = info[3 - sign] == 1
        ky_kind = jnp.zeros((cells_x, LANES), jnp.int32)
        for x in range(cells_x):
            ky_kind = jnp.where(cell == (x if sign else cells_x - 1 - x), kindy[side, x], ky_kind)
        fy_wide = jnp.broadcast_to(fy[sign], (cells_x, LANES))
        for at in range(per_sign):
            block = sign * per_sign + at
            ix, iy = lane_ints(first_ky, sign, at * LANES, (8, LANES))
            maxwell = jnp.exp((ix * ix + iy * iy).astype(F32) * (-UNIT * UNIT / 2.0))
            ghost = jnp.where(kx[sign] == 1.0, xw[block], column * maxwell[0:1])
            g[block, 0, 8:, :] = jnp.where(x_wall, ghost, xin(block))
            ghost_y = jnp.where(ky_kind == 1, yw[block], fy_wide * maxwell)
            value = jnp.where(y_wall, ghost_y, yin(block))
            for x in range(cells_x):
                g[block, 1 + x, 7:8, :] = value[x : x + 1]


def sweep(info, g, s, r, part="all"):
    blocks, slots, padded, _ = g.shape
    cells_x, cells_y = slots - 1, padded - 8
    tile = 16
    inner = [(x, at) for x in range(cells_x - 1, 0, -1) for at in range(cells_y - tile, 0, -tile)]
    rim = [(x, 0) for x in range(cells_x - 1, 0, -1)] + [(0, at) for at in range(cells_y - tile, -1, -tile)]
    todo = inner if part == "inner" else rim if part == "rim" else inner + rim

    def step(both, carry):
        for i in range(2):
            block = 2 * both + i
            half = slice(i * LANES, (i + 1) * LANES)
            ax, ay = block_speeds(info[0], block, blocks // 2, (tile, LANES))
            for x, at in todo:
                here = pl.ds(at, tile)
                value = s[block, x, here, :] + ax * g[block, x, pl.ds(8 + at, tile), :]
                value += ay * g[block, 1 + x, pl.ds(7 + at, tile), :]
                value = (value * r[both, x, here, half]).astype(BF16)
                g[block, 1 + x, pl.ds(8 + at, tile), :] = value.astype(F32)
        return carry

    lax.fori_loop(0, blocks // 2, step, 0)


def inner_kernel(s, r, g_in, g):
    blocks = g.shape[0]
    sweep(device_info(blocks // 2 * LANES // HALF), g, s, r, "inner")


def send_out(info, g, xmsg, ymsg, flux):
    blocks, slots, padded, _ = g.shape
    cells_x, cells_y = slots - 1, padded - 8
    per_sign = blocks // 2
    fx = None
    for sign in range(2):
        total = jnp.zeros((cells_y, LANES), F32)
        total_y = jnp.zeros((cells_x, LANES), F32)
        for at in range(per_sign):
            block = sign * per_sign + at
            ix, iy = lane_ints(info[0], sign, at * LANES, (8, LANES))
            ix, iy = jnp.abs(ix).astype(F32), jnp.abs(iy).astype(F32)
            row = g[block, cells_x, 8:, :]
            total += row * ix[0:1]
            edge = jnp.concatenate([g[block, 1 + x, padded - 1 : padded, :] for x in range(cells_x)], axis=0)
            ymsg[block] = edge.astype(BF16)
            total_y += edge * iy
        for at in range(per_sign):
            take = sign * (1 - info[5]) + (1 - sign) * info[5]
            xmsg[sign][at] = g[take * per_sign + at, cells_x, 8:, :].astype(BF16)
        pick = (iota((16, 3 * LANES), 0) == sign).astype(F32).astype(BF16)
        part = nt(pick, jnp.concatenate(pieces(total), axis=1).astype(BF16))[0:8]
        fx = part if fx is None else fx + part
        flux[2 - sign] = total_y
    flux[0] = fx


def spread(table, choice, size):
    row = iota((3 * size, choice.shape[1]), 0) % size
    return nn(table, (row == choice).astype(F32).astype(BF16))


def transposed(flip, table, ref, x, cells_x, cells_y):
    wide = nt(flip, stacked(table)).astype(BF16)
    ref[1, x * cells_y : (x + 1) * cells_y, :] = wide
    ref[0, (cells_x - 1 - x) * cells_y : (cells_x - x) * cells_y, :] = wide


def table_kernel(relax, kindx, pt, lri, bti, g, r, xw, yw, kx, tr):
    cells_x, _, count, cells_y = pt.shape
    per_sign = count // LANES
    info = device_info(count // HALF)
    flip = flip_matrix(info[1] == 1, cells_y).astype(BF16)
    base = 1.0 / TIME_STEP + 1.0 / relax[...]
    steps = iota((NVX, cells_y), 0).astype(F32) * STEP
    for x in range(cells_x):
        transposed(flip, 1.0 / (base[x : x + 1] + steps), tr, x, cells_x, cells_y)
    kind = jnp.concatenate([kindx[1:2], kindx[0:1], jnp.zeros((6, cells_y), jnp.int32)], axis=0).astype(F32)
    kind = nt(kind.astype(BF16), flip).astype(BF16)
    for sign in range(2):
        kx[sign] = tn(kind, (iota((8, LANES), 0) == sign).astype(F32).astype(BF16))
        for at in range(per_sign):
            block = sign * per_sign + at
            chunk = [2 * ((at * (LANES // HALF) + i) * NVX + HALF * sign) for i in range(LANES // HALF)]
            part = jnp.concatenate([lri[c : c + 2 * HALF, :] for c in chunk], axis=0)
            pick = (iota((LANES, 2 * LANES), 1) == 2 * iota((LANES, 2 * LANES), 0) + 1 - sign).astype(F32).astype(BF16)
            xw[block] = nt(flip, nn(pick, part).astype(BF16))
            part = jnp.concatenate([bti[c : c + 2 * HALF, :] for c in chunk], axis=0)
            row, col = iota((16, cells_x), 0), iota((16, cells_x), 1)
            order = (col == (row if sign else cells_x - 1 - row)).astype(F32).astype(BF16)
            pick = (iota((2 * LANES, LANES), 0) == 2 * iota((2 * LANES, LANES), 1) + 1 - info[1]).astype(F32).astype(BF16)
            yw[block] = nn(nt(order, part).astype(BF16), pick)[:cells_x]
        for at in range(0, per_sign, 2):
            ix, iy = lane_ints(info[0], sign, at * LANES, (1, 2 * LANES))
            both = (sign * per_sign + at) // 2
            r[both] = spread(tr[sign], (jnp.abs(ix) + jnp.abs(iy)) // 2, NVX).reshape(cells_x, cells_y, 2 * LANES)
            for xt in range(cells_x):
                x = xt if sign else cells_x - 1 - xt
                value = nt(flip, pt[x, sign, at * LANES : (at + 2) * LANES, :])
                for i in range(2):
                    g[2 * both + i, 1 + xt, 8:, :] = value[:, i * LANES : (i + 1) * LANES]


def first_kernel(kindy, same, other, relax, pair0, pair1, yrecv, xw, yw, kx, r, g_in,
                 g, s, xmsg0, xmsg1, ymsg, flux, ta, tb, fa, fb):
    blocks, slots, padded, _ = g.shape
    cells_x, cells_y = slots - 1, padded - 8
    per_sign = blocks // 2
    local_ky = per_sign * LANES // HALF
    info = device_info(local_ky)
    first_ky, up = info[0], info[1] == 1
    total = [same[q] + other[q] for q in range(4)]
    p = newton_params(total[0] * WEIGHT, total[1] * (WEIGHT * UNIT), total[2] * (WEIGHT * UNIT),
                      total[3] * (WEIGHT * UNIT * UNIT / 2.0))
    lead = p[0] - jnp.log(relax[...])
    flip = flip_matrix(up, cells_y).astype(BF16)
    vx = (2 * iota((NVX, cells_y), 0) - (NVX - 1)).astype(F32) * UNIT
    vy = (2 * (first_ky + iota((local_ky, cells_y), 0)) - (NVX - 1)).astype(F32) * UNIT
    half_p3 = p[3] * 0.5
    for x in range(cells_x):
        here = slice(x, x + 1)
        arg = vy * (p[2][here] + vy * half_p3[here])
        top = jnp.max(arg, axis=0, keepdims=True)
        transposed(flip, jnp.exp(arg - top), tb, x, cells_x, cells_y)
        arg = (lead[here] + top) + vx * (p[1][here] + vx * half_p3[here])
        transposed(flip, jnp.exp(arg), ta, x, cells_x, cells_y)
    for sign in range(2):
        fa[...] = spread(ta[sign], iota((1, LANES), 1) % HALF + HALF * sign, NVX)
        for at in range(0, per_sign, 2):
            block = sign * per_sign + at
            fb[...] = spread(tb[sign], iota((1, 2 * LANES), 1) // HALF + at * (LANES // HALF), local_ky)
            for xt in range(cells_x):
                here = slice(xt * cells_y, (xt + 1) * cells_y)
                for i in range(2):
                    maxwell = fa[here, :] * fb[here, i * LANES : (i + 1) * LANES]
                    s[block + i, xt] = g[block + i, 1 + xt, 8:, :] * (1.0 / TIME_STEP) + maxwell

    def xin(block):
        at = block % per_sign
        first = (info[5] == 1) == (block < per_sign)
        here = slice(at * LANES, (at + 1) * LANES)
        return nt(flip, jnp.where(first, pair0[here, :], pair1[here, :]))

    def yin(block):
        at = block % per_sign
        return yrecv[block // per_sign, :, at * LANES : (at + 1) * LANES].astype(F32)

    fill_inflow(info, kindy, same.at[4:7], other.at[4:7], g, xin, yin, xw, yw, kx)
    sweep(info, g, s, r)
    send_out(info, g, (xmsg0, xmsg1), ymsg, flux)


def next_kernel(last, kindy, same, other, pair0, pair1, yrecv, xw, yw, kx, s, r, g_in, *outs):
    blocks, slots, padded, _ = g_in.shape
    per_sign = blocks // 2
    info = device_info(per_sign * LANES // HALF)
    if last:
        out, g, rows, staged, sems = outs
    else:
        g, xmsg0, xmsg1, ymsg, flux = outs

    def xin(block):
        first = (info[5] == 1) == (block < per_sign)
        return jnp.where(first, pair0[block % per_sign].astype(F32), pair1[block % per_sign].astype(F32))

    def yin(block):
        return yrecv[block].astype(F32)

    fill_inflow(info, kindy, same, other, g, xin, yin, xw, yw, kx)
    sweep(info, g, s, r, "rim")
    if not last:
        send_out(info, g, (xmsg0, xmsg1), ymsg, flux)
        return
    cells_x, cells_y = slots - 1, padded - 8
    flip = flip_matrix(info[1] == 1, cells_y).astype(BF16)

    span = HALF * cells_x
    copies = []
    for sign in range(2):
        for at in range(per_sign):
            for x in range(cells_x):
                xt = x if sign else cells_x - 1 - x
                value = g[sign * per_sign + at, 1 + xt, 8:, :].astype(BF16)
                rows[pl.ds(x, LANES, stride=cells_x), :] = tn(value, flip)
            for i in range(LANES // HALF):
                chunk = (at * (LANES // HALF) + i) * 2 + sign
                staged[chunk * span : (chunk + 1) * span, :] = rows[i * span : (i + 1) * span, :].astype(BF16)
                copies.append(pltpu.make_async_copy(
                    staged.at[pl.ds(chunk * span, span), :], out.at[pl.ds(chunk * span, span), :], sems.at[chunk]))
                copies[-1].start()
    for copy in copies:
        copy.wait()


def call(kernel, outs, ins, smem=(), scratch=(), aliases=None, mib=20, far_in=(), far_out=(), cost=None):
    here = pl.BlockSpec(memory_space=pltpu.VMEM)
    scalar = pl.BlockSpec(memory_space=pltpu.SMEM)
    far = pl.BlockSpec(memory_space=pltpu.HBM)
    return pl.pallas_call(
        kernel,
        out_shape=outs,
        in_specs=[scalar if i in smem else far if i in far_in else here for i in range(len(ins))],
        out_specs=tuple(far if i in far_out else here for i in range(len(outs))),
        scratch_shapes=list(scratch),
        input_output_aliases=aliases or {},
        cost_estimate=cost,
        compiler_params=pltpu.CompilerParams(vmem_limit_bytes=mib << 20),
    )(*ins)


def body(previous, relax_time, left_right_kind, bottom_top_kind, left_right_inflow, bottom_top_inflow):
    vel_rows, cells_x, cells_y = previous.shape
    local_ky = vel_rows // NVX
    count = local_ky * HALF
    per_sign = count // LANES
    blocks = 2 * per_sign
    nvel, ngx, ngy = lax.axis_size("vel"), lax.axis_size("gx"), lax.axis_size("gy")
    def pairs(count, start):
        low = range(start, count - 1, 2)
        return [(i, i + 1) for i in low] + [(i + 1, i) for i in low]

    def swap_x(first, second):
        return lax.ppermute(first, "gx", pairs(ngx, 0)), lax.ppermute(second, "gx", pairs(ngx, 1))

    def swap_y(a):
        return lax.ppermute(a, "gy", pairs(ngy, 0))

    def sum_vel(a):
        reach = 1
        while reach < nvel // 2:
            a = a + lax.ppermute(a, "vel", [(i, i ^ reach) for i in range(nvel)])
            reach *= 2
        return a, lax.ppermute(a, "vel", [(i, i ^ reach) for i in range(nvel)])

    assert ngy == 2 and nvel & (nvel - 1) == 0, "mesh shape"
    sds = jax.ShapeDtypeStruct
    staging = [pltpu.VMEM((LANES * cells_x, cells_y), F32), pltpu.VMEM((vel_rows * cells_x, cells_y), BF16),
               pltpu.SemaphoreType.DMA((vel_rows // HALF,))]
    def far(a):
        return pltpu.with_memory_space_constraint(a, pltpu.HBM)

    pay, ymsg, pt, xmsg0, xmsg1, relax, kindx = call(
        moments_kernel,
        (sds((7, 8, LANES), F32), sds((2, cells_x, count), BF16), sds((cells_x, 2, count, cells_y), BF16),
         sds((count, cells_y), BF16), sds((count, cells_y), BF16), sds(relax_time.shape, F32), sds(left_right_kind.shape, jnp.int32)),
        (far(previous.reshape(vel_rows * cells_x, cells_y)), far(relax_time), far(left_right_kind)),
        scratch=staging + [pltpu.SemaphoreType.DMA((2,))], mib=10, far_in=(0, 1, 2))
    halo = swap_x(xmsg0, xmsg1)
    yrecv = swap_y(ymsg)
    sums = sum_vel(pay)
    lri = left_right_inflow.reshape(2 * vel_rows, cells_y)
    bti = bottom_top_inflow.reshape(2 * vel_rows, cells_x)
    g_shape = sds((blocks, cells_x + 1, cells_y + 8, LANES), F32)
    full = sds((blocks, cells_x, cells_y, LANES), F32)
    wide = sds((blocks // 2, cells_x, cells_y, 2 * LANES), F32)
    messages = (sds((per_sign, cells_y, LANES), BF16), sds((per_sign, cells_y, LANES), BF16),
                sds((blocks, cells_x, LANES), BF16), sds((3, 8, LANES), F32))
    work = pl.CostEstimate(flops=8 * vel_rows * cells_x * cells_y, bytes_accessed=16 * vel_rows * cells_x * cells_y, transcendentals=0)
    g, r, xw, yw, kx = call(
        table_kernel,
        (g_shape, wide, sds((blocks, cells_y, LANES), F32), sds((blocks, cells_x, LANES), F32), sds((2, cells_y, LANES), F32)),
        (relax, kindx, pt, lri, bti),
        scratch=[pltpu.VMEM((2, cells_x * cells_y, 3 * NVX), BF16)], mib=22, cost=work)
    g, s, xmsg0, xmsg1, ymsg, flux = call(
        first_kernel,
        (g_shape, full) + messages,
        (bottom_top_kind, *sums, relax, *halo, yrecv, xw, yw, kx, r, g), smem=(0,), aliases={11: 0},
        scratch=[
            pltpu.VMEM((2, cells_x * cells_y, 3 * NVX), BF16), pltpu.VMEM((2, cells_x * cells_y, 3 * local_ky), BF16),
            pltpu.VMEM((cells_x * cells_y, LANES), F32), pltpu.VMEM((cells_x * cells_y, 2 * LANES), F32)], mib=24)
    for number in range(1, SWEEPS):
        halo = swap_x(xmsg0, xmsg1)
        yrecv = swap_y(ymsg)
        sums = sum_vel(flux)
        g = call(inner_kernel, (g_shape,), (s, r, g), aliases={2: 0}, mib=20, cost=work)[0]
        ins = (bottom_top_kind, *sums, *halo, yrecv, xw, yw, kx, s, r, g)
        if number == SWEEPS - 1:
            out, _ = call(functools.partial(next_kernel, True),
                          (sds((vel_rows * cells_x, cells_y), BF16), g_shape), ins, smem=(0,), aliases={11: 1},
                          scratch=staging, mib=22, far_out=(0,))
        else:
            g, xmsg0, xmsg1, ymsg, flux = call(
                functools.partial(next_kernel, False), (g_shape,) + messages, ins, smem=(0,), aliases={11: 0}, mib=22)
    return out.reshape(vel_rows, cells_x, cells_y)


def solution(mesh):
    return jax.shard_map(
        body,
        mesh=mesh,
        in_specs=(P("vel", "gx", "gy"), P("gx", "gy"), P(None, "gy"), P(None, "gx"), P("vel", None, "gy"), P("vel", None, "gx")),
        out_specs=P("vel", "gx", "gy"),
        check_vma=False,
    )
```

```python
import functools
import math

import jax
import jax.numpy as jnp
import numpy as np
from jax import lax
from jax.experimental import pallas as pl
from jax.experimental.pallas import tpu as pltpu
from jax.sharding import PartitionSpec as P


NVX = 64
HALF = NVX // 2
NEWTON = 2
SWEEPS = 4
COURANT = 100.0
STEP = 12.0 / NVX
UNIT = STEP / 2.0
WEIGHT = STEP * STEP / (2.0 * math.pi)
TIME_STEP = COURANT / ((NVX - 1) * STEP)
LANES = 128
F32 = jnp.float32
BF16 = jnp.bfloat16


def wall_norm_value():
    line = (np.arange(NVX) - (NVX - 1) / 2.0) * STEP
    gauss = np.exp(-line * line / 2.0)
    return float(np.sum(np.maximum(line, 0.0) * gauss) * np.sum(gauss) * WEIGHT)


FLUX_SCALE = WEIGHT * UNIT / wall_norm_value()


def nn(a, b, precision=None):
    return lax.dot_general(a, b, (((1,), (0,)), ((), ())), precision=precision, preferred_element_type=F32)


def nt(a, b, precision=None):
    return lax.dot_general(a, b, (((1,), (1,)), ((), ())), precision=precision, preferred_element_type=F32)


def tn(a, b, precision=None):
    return lax.dot_general(a, b, (((0,), (0,)), ((), ())), precision=precision, preferred_element_type=F32)


def iota(shape, dim):
    return lax.broadcasted_iota(jnp.int32, shape, dim)


def lane_ints(first_ky, sign, start, shape):
    lane = iota(shape, len(shape) - 1) + start
    ix = 2 * (lane % HALF + HALF * sign) - (NVX - 1)
    iy = 2 * (first_ky + lane // HALF) - (NVX - 1)
    return ix, iy


def device_info(local_ky):
    v, ix, iy = lax.axis_index("vel"), lax.axis_index("gx"), lax.axis_index("gy")
    up = (v >= lax.axis_size("vel") // 2).astype(jnp.int32)
    wall = jnp.where(iy == jnp.where(up == 1, 0, lax.axis_size("gy") - 1), 1, 0)
    first, last = (ix == 0).astype(jnp.int32), (ix == lax.axis_size("gx") - 1).astype(jnp.int32)
    return [v * local_ky, up, first, last, wall, 1 - lax.rem(ix, 2)]


def flip_matrix(up, size):
    row, col = iota((size, size), 0), iota((size, size), 1)
    return (col == jnp.where(up, row, size - 1 - row)).astype(F32)


def reverse_rows(a):
    return jnp.concatenate([a[i : i + 1] for i in range(a.shape[0] - 1, -1, -1)], axis=0)


def pieces(a):
    high = a.astype(BF16).astype(F32)
    rest = a - high
    middle = rest.astype(BF16).astype(F32)
    return [high, middle, rest - middle]


def stacked(a):
    return jnp.concatenate(pieces(a), axis=0).astype(BF16)


def moments_kernel(prev, relax_far, kindx_far, lri_far, bti_far, pay, ymsg, pt, xmsg0, xmsg1, relax, kindx, lri, bti, rows, staged, sems, few):
    cells_x, _, count, cells_y = pt.shape
    info = device_info(count // HALF)
    span = HALF * cells_x
    copies = [pltpu.make_async_copy(prev.at[pl.ds(i * span, span), :], staged.at[pl.ds(i * span, span), :], sems.at[i])
              for i in range(2 * count // HALF)]
    order = [2 * i + sign for sign in range(2) for i in range(count // HALF)]
    for i in order:
        copies[i].start()
    small = [pltpu.make_async_copy(source, target, few.at[i]) for i, (source, target) in enumerate(
        ((relax_far, relax), (kindx_far, kindx), (lri_far, lri), (bti_far, bti)))]
    for copy in small:
        copy.start()
    for sign in range(2):
        for at in range(count // LANES):
            for i in range(LANES // HALF):
                chunk = (at * (LANES // HALF) + i) * 2 + sign
                copies[chunk].wait()
                rows[i * span : (i + 1) * span, :] = staged[chunk * span : (chunk + 1) * span, :].astype(F32)
            for x in range(cells_x):
                pt[x, sign, at * LANES : (at + 1) * LANES, :] = rows[pl.ds(x, LANES, stride=cells_x), :].astype(BF16)
    even = info[5]
    xmsg0[...] = pt[(cells_x - 1) * even, even]
    xmsg1[...] = pt[(cells_x - 1) * (1 - even), 1 - even]
    first_ky, up = info[0], info[1] == 1
    y_out = jnp.where(up, cells_y - 1, 0)
    row = iota((16, count), 0)
    weights = []
    for sign in range(2):
        ix, iy = lane_ints(first_ky, sign, 0, (16, count))
        energy = ix * ix + iy * iy
        low = energy % 64
        table = jnp.where(row == 0, 1, jnp.where(row == 1, ix, jnp.where(row == 2, iy, jnp.where(
            row == 3, energy - low, jnp.where(row == 4, low, jnp.where(row == 5, jnp.abs(ix), 0))))))
        weights.append(table.astype(F32).astype(BF16))
    edge = [jnp.zeros((16, count), F32) for _ in range(2)]
    out_row = [None, None]
    pick_row, pick_col = iota((16, cells_y), 0), iota((16, cells_y), 1)
    for x in range(cells_x):
        total = None
        for sign in range(2):
            block = pt[x, sign]
            part = nn(weights[sign], block)
            if x == (cells_x - 1) * sign:
                out_row[sign] = part[5:6]
            total = part if total is None else total + part
            at = x if sign else cells_x - 1 - x
            pick = ((pick_row == at) & (pick_col == y_out)).astype(F32).astype(BF16)
            edge[sign] = edge[sign] + nt(pick, block)
        pay[0, x : x + 1, :] = total[0:1]
        pay[1, x : x + 1, :] = total[1:2]
        pay[2, x : x + 1, :] = total[2:3]
        pay[3, x : x + 1, :] = total[3:4] + total[4:5]
    flip = flip_matrix(up, cells_y)
    fx = jnp.concatenate([out_row[0], out_row[1], jnp.zeros((6, cells_y), F32)], axis=0)
    turned = nt(stacked(fx), flip.astype(BF16))
    pay[4] = turned[0:8] + turned[8:16] + turned[16:24]
    for sign in range(2):
        total = jnp.zeros((cells_x, LANES), F32)
        for at in range(count // LANES):
            _, iy = lane_ints(first_ky, sign, at * LANES, (cells_x, LANES))
            total += jnp.abs(iy).astype(F32) * edge[sign][:cells_x, at * LANES : (at + 1) * LANES]
        pay[6 - sign] = total
        ymsg[sign] = edge[sign][:cells_x].astype(BF16)
    for copy in small:
        copy.wait()


def newton_params(u0, u1, u2, u3):
    ux, uy = u1 / u0, u2 / u0
    square = ux * ux + uy * uy
    temperature = u3 / u0 - square / 2.0
    p = [jnp.log(u0 / temperature) - square / (2.0 * temperature), ux / temperature, uy / temperature, -1.0 / temperature]
    last = (HALF - 0.5) * STEP
    for _ in range(NEWTON):
        half_p3 = p[3] * 0.5
        sums, tops = [], []
        for slope in (p[1], p[2]):
            vertex = jnp.where(p[3] < 0.0, -slope / p[3], 0.0) * (1.0 / STEP)
            node = (jnp.clip(jnp.floor(vertex), -HALF, HALF - 1.0) + 0.5) * STEP
            end = (last * last) * half_p3 + last * jnp.abs(slope)
            top = jnp.maximum(node * (slope + node * half_p3), end)
            total = [None] * 5
            for i in range(HALF):
                value = (i + 0.5) * STEP
                even, odd = (value * value) * half_p3 - top, value * slope
                plus, minus = jnp.exp(even + odd), jnp.exp(even - odd)
                even, odd = plus + minus, plus - minus
                terms = [even, value * odd, value**2 * even, value**3 * odd, value**4 * even]
                total = [t if old is None else old + t for old, t in zip(total, terms)]
            sums.append(total)
            tops.append(top)
        scale = jnp.exp(p[0] + (tops[0] + tops[1])) * WEIGHT
        x = sums[0]
        y = [scale * t for t in sums[1]]
        x2, y2 = x[2] * y[0], x[0] * y[2]
        n = [x[0] * y[0], x[1] * y[0], x[0] * y[1], (x2 + y2) * 0.5, x2, x[1] * y[1],
             (x[3] * y[0] + x[1] * y[2]) * 0.5, y2, (x[2] * y[1] + x[0] * y[3]) * 0.5,
             (x[4] * y[0] + 2.0 * (x[2] * y[2]) + x[0] * y[4]) * 0.25]
        layout = [[0, 1, 2, 3], [1, 4, 5, 6], [2, 5, 7, 8], [3, 6, 8, 9]]
        matrix = [[n[layout[r][c]] for c in range(4)] for r in range(4)]
        target = [n[0] - u0, n[1] - u1, n[2] - u2, n[3] - u3]
        for pivot in range(4):
            for lower in range(pivot + 1, 4):
                factor = matrix[lower][pivot] / matrix[pivot][pivot]
                for col in range(pivot, 4):
                    matrix[lower][col] = matrix[lower][col] - factor * matrix[pivot][col]
                target[lower] = target[lower] - factor * target[pivot]
        result = [None] * 4
        for pivot in (3, 2, 1, 0):
            accum = target[pivot]
            for col in range(pivot + 1, 4):
                accum = accum - matrix[pivot][col] * result[col]
            result[pivot] = accum / matrix[pivot][pivot]
        p = [a - b for a, b in zip(p, result)]
    return p


def block_speeds(first_ky, block, per_sign, shape):
    ix, iy = lane_ints(first_ky, block // per_sign, (block % per_sign) * LANES, shape)
    return jnp.abs(ix).astype(F32) * UNIT, jnp.abs(iy).astype(F32) * UNIT


def fill_inflow(info, kindy, same, other, g, xin, yin, xw, yw, kx):
    blocks, slots, padded, _ = g.shape
    cells_x, cells_y = slots - 1, padded - 8
    per_sign = blocks // 2
    first_ky, up = info[0], info[1] == 1
    anti = flip_matrix(False, cells_y)
    turned = nn(stacked(other[0]), anti.astype(BF16))
    fx = (same[0] + (turned[0:8] + turned[8:16] + turned[16:24])) * FLUX_SCALE
    lane = iota((24, 2 * LANES), 1) // LANES
    columns = tn(stacked(fx), (iota((24, 2 * LANES), 0) % 8 == 1 - lane).astype(F32).astype(BF16))
    fy = jnp.sum(other[1], axis=1, keepdims=True) + reverse_rows(jnp.sum(other[2], axis=1, keepdims=True))
    fy = fy * FLUX_SCALE
    fy = [reverse_rows(fy), fy]
    side = jnp.where(up, 0, 1)
    cell = iota((cells_x, LANES), 0)
    y_wall = info[4] == 1
    for sign in range(2):
        column = columns[:, sign * LANES : (sign + 1) * LANES]
        x_wall = info[3 - sign] == 1
        ky_kind = jnp.zeros((cells_x, LANES), jnp.int32)
        for x in range(cells_x):
            ky_kind = jnp.where(cell == (x if sign else cells_x - 1 - x), kindy[side, x], ky_kind)
        fy_wide = jnp.broadcast_to(fy[sign], (cells_x, LANES))
        for at in range(per_sign):
            block = sign * per_sign + at
            ix, iy = lane_ints(first_ky, sign, at * LANES, (8, LANES))
            maxwell = jnp.exp((ix * ix + iy * iy).astype(F32) * (-UNIT * UNIT / 2.0))
            ghost = jnp.where(kx[sign] == 1.0, xw[block], column * maxwell[0:1])
            g[block, 0, 8:, :] = jnp.where(x_wall, ghost, xin(block))
            ghost_y = jnp.where(ky_kind == 1, yw[block], fy_wide * maxwell)
            value = jnp.where(y_wall, ghost_y, yin(block))
            for x in range(cells_x):
                g[block, 1 + x, 7:8, :] = value[x : x + 1]


def sweep(info, g, s, r, part="all"):
    blocks, slots, padded, _ = g.shape
    cells_x, cells_y = slots - 1, padded - 8
    tile = 16
    inner = [(x, at) for x in range(cells_x - 1, 0, -1) for at in range(cells_y - tile, 0, -tile)]
    rim = [(x, 0) for x in range(cells_x - 1, 0, -1)] + [(0, at) for at in range(cells_y - tile, -1, -tile)]
    todo = inner if part == "inner" else rim if part == "rim" else inner + rim

    def step(both, carry):
        for i in range(2):
            block = 2 * both + i
            half = slice(i * LANES, (i + 1) * LANES)
            ax, ay = block_speeds(info[0], block, blocks // 2, (tile, LANES))
            for x, at in todo:
                here = pl.ds(at, tile)
                value = s[block, x, here, :] + ax * g[block, x, pl.ds(8 + at, tile), :]
                value += ay * g[block, 1 + x, pl.ds(7 + at, tile), :]
                value = (value * r[both, x, here, half]).astype(BF16)
                g[block, 1 + x, pl.ds(8 + at, tile), :] = value.astype(F32)
        return carry

    lax.fori_loop(0, blocks // 2, step, 0)


def inner_kernel(s, r, g_in, g):
    blocks = g.shape[0]
    sweep(device_info(blocks // 2 * LANES // HALF), g, s, r, "inner")


def send_out(info, g, xmsg, ymsg, flux):
    blocks, slots, padded, _ = g.shape
    cells_x, cells_y = slots - 1, padded - 8
    per_sign = blocks // 2
    fx = None
    for sign in range(2):
        total = jnp.zeros((cells_y, LANES), F32)
        total_y = jnp.zeros((cells_x, LANES), F32)
        for at in range(per_sign):
            block = sign * per_sign + at
            ix, iy = lane_ints(info[0], sign, at * LANES, (8, LANES))
            ix, iy = jnp.abs(ix).astype(F32), jnp.abs(iy).astype(F32)
            row = g[block, cells_x, 8:, :]
            total += row * ix[0:1]
            edge = jnp.concatenate([g[block, 1 + x, padded - 1 : padded, :] for x in range(cells_x)], axis=0)
            ymsg[block] = edge.astype(BF16)
            total_y += edge * iy
        for at in range(per_sign):
            take = sign * (1 - info[5]) + (1 - sign) * info[5]
            xmsg[sign][at] = g[take * per_sign + at, cells_x, 8:, :].astype(BF16)
        pick = (iota((16, 3 * LANES), 0) == sign).astype(F32).astype(BF16)
        part = nt(pick, jnp.concatenate(pieces(total), axis=1).astype(BF16))[0:8]
        fx = part if fx is None else fx + part
        flux[2 - sign] = total_y
    flux[0] = fx


def spread(table, choice, size):
    row = iota((3 * size, choice.shape[1]), 0) % size
    return nn(table, (row == choice).astype(F32).astype(BF16))


def transposed(flip, table, ref, x, cells_x, cells_y):
    wide = nt(flip, stacked(table)).astype(BF16)
    ref[1, x * cells_y : (x + 1) * cells_y, :] = wide
    ref[0, (cells_x - 1 - x) * cells_y : (cells_x - x) * cells_y, :] = wide


def table_kernel(relax, kindx, pt, lri, bti, g, r, xw, yw, kx, tr):
    cells_x, _, count, cells_y = pt.shape
    per_sign = count // LANES
    info = device_info(count // HALF)
    flip = flip_matrix(info[1] == 1, cells_y).astype(BF16)
    base = 1.0 / TIME_STEP + 1.0 / relax[...]
    steps = iota((NVX, cells_y), 0).astype(F32) * STEP
    for x in range(cells_x):
        transposed(flip, 1.0 / (base[x : x + 1] + steps), tr, x, cells_x, cells_y)
    kind = jnp.concatenate([kindx[1:2], kindx[0:1], jnp.zeros((6, cells_y), jnp.int32)], axis=0).astype(F32)
    kind = nt(kind.astype(BF16), flip).astype(BF16)
    for sign in range(2):
        kx[sign] = tn(kind, (iota((8, LANES), 0) == sign).astype(F32).astype(BF16))
        for at in range(per_sign):
            block = sign * per_sign + at
            chunk = [2 * ((at * (LANES // HALF) + i) * NVX + HALF * sign) for i in range(LANES // HALF)]
            part = jnp.concatenate([lri[c : c + 2 * HALF, :] for c in chunk], axis=0)
            pick = (iota((LANES, 2 * LANES), 1) == 2 * iota((LANES, 2 * LANES), 0) + 1 - sign).astype(F32).astype(BF16)
            xw[block] = nt(flip, nn(pick, part).astype(BF16))
            row, col = iota((16, cells_x), 0), iota((16, cells_x), 1)
            order = (col == (row if sign else cells_x - 1 - row)).astype(F32).astype(BF16)
            part = nn(order, bti[1 - info[1], :, at * 2 * LANES : (at + 1) * 2 * LANES]).astype(BF16)
            row, col = iota((2 * LANES, LANES), 0), iota((2 * LANES, LANES), 1)
            pick = (row == col // HALF * NVX + HALF * sign + col % HALF).astype(F32).astype(BF16)
            yw[block] = nn(part, pick)[:cells_x]
        for at in range(0, per_sign, 2):
            ix, iy = lane_ints(info[0], sign, at * LANES, (1, 2 * LANES))
            both = (sign * per_sign + at) // 2
            r[both] = spread(tr[sign], (jnp.abs(ix) + jnp.abs(iy)) // 2, NVX).reshape(cells_x, cells_y, 2 * LANES)
            for xt in range(cells_x):
                x = xt if sign else cells_x - 1 - xt
                value = nt(flip, pt[x, sign, at * LANES : (at + 2) * LANES, :])
                for i in range(2):
                    g[2 * both + i, 1 + xt, 8:, :] = value[:, i * LANES : (i + 1) * LANES]


def first_kernel(kindy, same, other, relax, pair0, pair1, yrecv, xw, yw, kx, r, g_in,
                 g, s, xmsg0, xmsg1, ymsg, flux, ta, tb, fa, fb):
    blocks, slots, padded, _ = g.shape
    cells_x, cells_y = slots - 1, padded - 8
    per_sign = blocks // 2
    local_ky = per_sign * LANES // HALF
    info = device_info(local_ky)
    first_ky, up = info[0], info[1] == 1
    total = [same[q] + other[q] for q in range(4)]
    p = newton_params(total[0] * WEIGHT, total[1] * (WEIGHT * UNIT), total[2] * (WEIGHT * UNIT),
                      total[3] * (WEIGHT * UNIT * UNIT / 2.0))
    lead = p[0] - jnp.log(relax[...])
    flip = flip_matrix(up, cells_y).astype(BF16)
    vx = (2 * iota((NVX, cells_y), 0) - (NVX - 1)).astype(F32) * UNIT
    vy = (2 * (first_ky + iota((local_ky, cells_y), 0)) - (NVX - 1)).astype(F32) * UNIT
    half_p3 = p[3] * 0.5
    for x in range(cells_x):
        here = slice(x, x + 1)
        arg = vy * (p[2][here] + vy * half_p3[here])
        top = jnp.max(arg, axis=0, keepdims=True)
        transposed(flip, jnp.exp(arg - top), tb, x, cells_x, cells_y)
        arg = (lead[here] + top) + vx * (p[1][here] + vx * half_p3[here])
        transposed(flip, jnp.exp(arg), ta, x, cells_x, cells_y)
    for sign in range(2):
        fa[...] = spread(ta[sign], iota((1, LANES), 1) % HALF + HALF * sign, NVX)
        for at in range(0, per_sign, 2):
            block = sign * per_sign + at
            fb[...] = spread(tb[sign], iota((1, 2 * LANES), 1) // HALF + at * (LANES // HALF), local_ky)
            for xt in range(cells_x):
                here = slice(xt * cells_y, (xt + 1) * cells_y)
                for i in range(2):
                    maxwell = fa[here, :] * fb[here, i * LANES : (i + 1) * LANES]
                    s[block + i, xt] = g[block + i, 1 + xt, 8:, :] * (1.0 / TIME_STEP) + maxwell

    def xin(block):
        at = block % per_sign
        first = (info[5] == 1) == (block < per_sign)
        here = slice(at * LANES, (at + 1) * LANES)
        return nt(flip, jnp.where(first, pair0[here, :], pair1[here, :]))

    def yin(block):
        at = block % per_sign
        return yrecv[block // per_sign, :, at * LANES : (at + 1) * LANES].astype(F32)

    fill_inflow(info, kindy, same.at[4:7], other.at[4:7], g, xin, yin, xw, yw, kx)
    sweep(info, g, s, r)
    send_out(info, g, (xmsg0, xmsg1), ymsg, flux)


def next_kernel(last, kindy, same, other, pair0, pair1, yrecv, xw, yw, kx, s, r, g_in, *outs):
    blocks, slots, padded, _ = g_in.shape
    per_sign = blocks // 2
    info = device_info(per_sign * LANES // HALF)
    if last:
        out, g, rows, staged, sems = outs
    else:
        g, xmsg0, xmsg1, ymsg, flux = outs

    def xin(block):
        first = (info[5] == 1) == (block < per_sign)
        return jnp.where(first, pair0[block % per_sign].astype(F32), pair1[block % per_sign].astype(F32))

    def yin(block):
        return yrecv[block].astype(F32)

    fill_inflow(info, kindy, same, other, g, xin, yin, xw, yw, kx)
    sweep(info, g, s, r, "rim")
    if not last:
        send_out(info, g, (xmsg0, xmsg1), ymsg, flux)
        return
    cells_x, cells_y = slots - 1, padded - 8
    flip = flip_matrix(info[1] == 1, cells_y).astype(BF16)

    span = HALF * cells_x
    copies = []
    for sign in range(2):
        for at in range(per_sign):
            for x in range(cells_x):
                xt = x if sign else cells_x - 1 - x
                value = g[sign * per_sign + at, 1 + xt, 8:, :].astype(BF16)
                rows[pl.ds(x, LANES, stride=cells_x), :] = tn(value, flip)
            for i in range(LANES // HALF):
                chunk = (at * (LANES // HALF) + i) * 2 + sign
                staged[chunk * span : (chunk + 1) * span, :] = rows[i * span : (i + 1) * span, :].astype(BF16)
                copies.append(pltpu.make_async_copy(
                    staged.at[pl.ds(chunk * span, span), :], out.at[pl.ds(chunk * span, span), :], sems.at[chunk]))
                copies[-1].start()
    for copy in copies:
        copy.wait()


def call(kernel, outs, ins, smem=(), scratch=(), aliases=None, mib=20, far_in=(), far_out=(), cost=None):
    here = pl.BlockSpec(memory_space=pltpu.VMEM)
    scalar = pl.BlockSpec(memory_space=pltpu.SMEM)
    far = pl.BlockSpec(memory_space=pltpu.HBM)
    return pl.pallas_call(
        kernel,
        out_shape=outs,
        in_specs=[scalar if i in smem else far if i in far_in else here for i in range(len(ins))],
        out_specs=tuple(far if i in far_out else here for i in range(len(outs))),
        scratch_shapes=list(scratch),
        input_output_aliases=aliases or {},
        cost_estimate=cost,
        compiler_params=pltpu.CompilerParams(vmem_limit_bytes=mib << 20),
    )(*ins)


def body(previous, relax_time, left_right_kind, bottom_top_kind, left_right_inflow, bottom_top_inflow):
    vel_rows, cells_x, cells_y = previous.shape
    local_ky = vel_rows // NVX
    count = local_ky * HALF
    per_sign = count // LANES
    blocks = 2 * per_sign
    nvel, ngx, ngy = lax.axis_size("vel"), lax.axis_size("gx"), lax.axis_size("gy")

    def pairs(count, start):
        low = range(start, count - 1, 2)
        return [(i, i + 1) for i in low] + [(i + 1, i) for i in low]

    def exchange(first, second, edge, part):
        reach = 1
        while reach < nvel // 2:
            part = part + lax.ppermute(part, "vel", [(i, i ^ reach) for i in range(nvel)])
            reach *= 2
        other = lax.ppermute(part, "vel", [(i, i ^ reach) for i in range(nvel)])
        edge = lax.ppermute(edge, "gy", pairs(ngy, 0))
        first = lax.ppermute(first, "gx", pairs(ngx, 0))
        second = lax.ppermute(second, "gx", pairs(ngx, 1))
        return (first, second), edge, (part, other)

    assert ngy == 2 and nvel & (nvel - 1) == 0, "mesh shape"
    sds = jax.ShapeDtypeStruct
    staging = [pltpu.VMEM((LANES * cells_x, cells_y), F32), pltpu.VMEM((vel_rows * cells_x, cells_y), BF16),
               pltpu.SemaphoreType.DMA((vel_rows // HALF,))]

    def far(a):
        return pltpu.with_memory_space_constraint(a, pltpu.HBM)

    pay, ymsg, pt, xmsg0, xmsg1, relax, kindx, lri, bti = call(
        moments_kernel,
        (sds((7, 8, LANES), F32), sds((2, cells_x, count), BF16), sds((cells_x, 2, count, cells_y), BF16),
         sds((count, cells_y), BF16), sds((count, cells_y), BF16), sds(relax_time.shape, F32), sds(left_right_kind.shape, jnp.int32),
         sds((2 * vel_rows, cells_y), BF16), sds((2, cells_x, vel_rows), BF16)),
        (far(previous.reshape(vel_rows * cells_x, cells_y)), far(relax_time), far(left_right_kind),
         far(left_right_inflow.reshape(2 * vel_rows, cells_y)), far(bottom_top_inflow.transpose(1, 2, 0))),
        scratch=staging + [pltpu.SemaphoreType.DMA((4,))], mib=10, far_in=(0, 1, 2, 3, 4))
    halo, yrecv, sums = exchange(xmsg0, xmsg1, ymsg, pay)
    g_shape = sds((blocks, cells_x + 1, cells_y + 8, LANES), F32)
    full = sds((blocks, cells_x, cells_y, LANES), F32)
    wide = sds((blocks // 2, cells_x, cells_y, 2 * LANES), F32)
    messages = (sds((per_sign, cells_y, LANES), BF16), sds((per_sign, cells_y, LANES), BF16),
                sds((blocks, cells_x, LANES), BF16), sds((3, 8, LANES), F32))
    work = pl.CostEstimate(flops=8 * vel_rows * cells_x * cells_y, bytes_accessed=16 * vel_rows * cells_x * cells_y, transcendentals=0)
    g, r, xw, yw, kx = call(
        table_kernel,
        (g_shape, wide, sds((blocks, cells_y, LANES), F32), sds((blocks, cells_x, LANES), F32), sds((2, cells_y, LANES), F32)),
        (relax, kindx, pt, lri, bti),
        scratch=[pltpu.VMEM((2, cells_x * cells_y, 3 * NVX), BF16)], mib=22, cost=work)
    g, s, xmsg0, xmsg1, ymsg, flux = call(
        first_kernel,
        (g_shape, full) + messages,
        (bottom_top_kind, *sums, relax, *halo, yrecv, xw, yw, kx, r, g), smem=(0,), aliases={11: 0},
        scratch=[
            pltpu.VMEM((2, cells_x * cells_y, 3 * NVX), BF16), pltpu.VMEM((2, cells_x * cells_y, 3 * local_ky), BF16),
            pltpu.VMEM((cells_x * cells_y, LANES), F32), pltpu.VMEM((cells_x * cells_y, 2 * LANES), F32)], mib=24)
    for number in range(1, SWEEPS):
        halo, yrecv, sums = exchange(xmsg0, xmsg1, ymsg, flux)
        g = call(inner_kernel, (g_shape,), (s, r, g), aliases={2: 0}, mib=20, cost=work)[0]
        ins = (bottom_top_kind, *sums, *halo, yrecv, xw, yw, kx, s, r, g)
        if number == SWEEPS - 1:
            out, _ = call(functools.partial(next_kernel, True),
                          (sds((vel_rows * cells_x, cells_y), BF16), g_shape), ins, smem=(0,), aliases={11: 1},
                          scratch=staging, mib=22, far_out=(0,))
        else:
            g, xmsg0, xmsg1, ymsg, flux = call(
                functools.partial(next_kernel, False), (g_shape,) + messages, ins, smem=(0,), aliases={11: 0}, mib=22)
    return out.reshape(vel_rows, cells_x, cells_y)


def solution(mesh):
    return jax.shard_map(
        body,
        mesh=mesh,
        in_specs=(P("vel", "gx", "gy"), P("gx", "gy"), P(None, "gy"), P(None, "gx"), P("vel", None, "gy"), P("vel", None, "gx")),
        out_specs=P("vel", "gx", "gy"),
        check_vma=False,
    )
```

```python
import functools
import math

import jax
import jax.numpy as jnp
import numpy as np
from jax import lax
from jax.experimental import pallas as pl
from jax.experimental.pallas import tpu as pltpu
from jax.sharding import PartitionSpec as P


NVX = 64
HALF = NVX // 2
NEWTON = 2
SWEEPS = 4
COURANT = 100.0
STEP = 12.0 / NVX
UNIT = STEP / 2.0
WEIGHT = STEP * STEP / (2.0 * math.pi)
TIME_STEP = COURANT / ((NVX - 1) * STEP)
LANES = 128
F32 = jnp.float32
BF16 = jnp.bfloat16


def wall_norm_value():
    line = (np.arange(NVX) - (NVX - 1) / 2.0) * STEP
    gauss = np.exp(-line * line / 2.0)
    return float(np.sum(np.maximum(line, 0.0) * gauss) * np.sum(gauss) * WEIGHT)


FLUX_SCALE = WEIGHT * UNIT / wall_norm_value()


def nn(a, b, precision=None):
    return lax.dot_general(a, b, (((1,), (0,)), ((), ())), precision=precision, preferred_element_type=F32)


def nt(a, b, precision=None):
    return lax.dot_general(a, b, (((1,), (1,)), ((), ())), precision=precision, preferred_element_type=F32)


def tn(a, b, precision=None):
    return lax.dot_general(a, b, (((0,), (0,)), ((), ())), precision=precision, preferred_element_type=F32)


def iota(shape, dim):
    return lax.broadcasted_iota(jnp.int32, shape, dim)


def lane_ints(first_ky, sign, start, shape):
    lane = iota(shape, len(shape) - 1) + start
    ix = 2 * (lane % HALF + HALF * sign) - (NVX - 1)
    iy = 2 * (first_ky + lane // HALF) - (NVX - 1)
    return ix, iy


def device_info(local_ky):
    v, ix, iy = lax.axis_index("vel"), lax.axis_index("gx"), lax.axis_index("gy")
    up = (v >= lax.axis_size("vel") // 2).astype(jnp.int32)
    wall = jnp.where(iy == jnp.where(up == 1, 0, lax.axis_size("gy") - 1), 1, 0)
    first, last = (ix == 0).astype(jnp.int32), (ix == lax.axis_size("gx") - 1).astype(jnp.int32)
    return [v * local_ky, up, first, last, wall, 1 - lax.rem(ix, 2)]


def flip_matrix(up, size):
    row, col = iota((size, size), 0), iota((size, size), 1)
    return (col == jnp.where(up, row, size - 1 - row)).astype(F32)


def reverse_rows(a):
    return jnp.concatenate([a[i : i + 1] for i in range(a.shape[0] - 1, -1, -1)], axis=0)


def pieces(a):
    high = a.astype(BF16).astype(F32)
    rest = a - high
    middle = rest.astype(BF16).astype(F32)
    return [high, middle, rest - middle]


def stacked(a):
    return jnp.concatenate(pieces(a), axis=0).astype(BF16)


def moments_kernel(prev, relax_far, kindx_far, kindy_far, lri_far, bti_far, pay, ymsg, pt, xmsg0, xmsg1, relax, kindx, kindy, lri, bti, rows, staged, sems, few):
    cells_x, _, count, cells_y = pt.shape
    info = device_info(count // HALF)
    span = HALF * cells_x
    copies = [pltpu.make_async_copy(prev.at[pl.ds(i * span, span), :], staged.at[pl.ds(i * span, span), :], sems.at[i])
              for i in range(2 * count // HALF)]
    order = [2 * i + sign for sign in range(2) for i in range(count // HALF)]
    for i in order:
        copies[i].start()
    small = [pltpu.make_async_copy(source, target, few.at[i]) for i, (source, target) in enumerate(
        ((relax_far, relax), (kindx_far, kindx), (kindy_far, kindy), (lri_far, lri), (bti_far, bti)))]
    for copy in small:
        copy.start()
    for sign in range(2):
        for at in range(count // LANES):
            for i in range(LANES // HALF):
                chunk = (at * (LANES // HALF) + i) * 2 + sign
                copies[chunk].wait()
                rows[i * span : (i + 1) * span, :] = staged[chunk * span : (chunk + 1) * span, :].astype(F32)
            for x in range(cells_x):
                pt[x, sign, at * LANES : (at + 1) * LANES, :] = rows[pl.ds(x, LANES, stride=cells_x), :].astype(BF16)
    even = info[5]
    xmsg0[...] = pt[(cells_x - 1) * even, even]
    xmsg1[...] = pt[(cells_x - 1) * (1 - even), 1 - even]
    first_ky, up = info[0], info[1] == 1
    y_out = jnp.where(up, cells_y - 1, 0)
    row = iota((16, count), 0)
    weights = []
    for sign in range(2):
        ix, iy = lane_ints(first_ky, sign, 0, (16, count))
        energy = ix * ix + iy * iy
        low = energy % 64
        table = jnp.where(row == 0, 1, jnp.where(row == 1, ix, jnp.where(row == 2, iy, jnp.where(
            row == 3, energy - low, jnp.where(row == 4, low, jnp.where(row == 5, jnp.abs(ix), 0))))))
        weights.append(table.astype(F32).astype(BF16))
    edge = [jnp.zeros((16, count), F32) for _ in range(2)]
    out_row = [None, None]
    pick_row, pick_col = iota((16, cells_y), 0), iota((16, cells_y), 1)
    for x in range(cells_x):
        total = None
        for sign in range(2):
            block = pt[x, sign]
            part = nn(weights[sign], block)
            if x == (cells_x - 1) * sign:
                out_row[sign] = part[5:6]
            total = part if total is None else total + part
            at = x if sign else cells_x - 1 - x
            pick = ((pick_row == at) & (pick_col == y_out)).astype(F32).astype(BF16)
            edge[sign] = edge[sign] + nt(pick, block)
        pay[0, x : x + 1, :] = total[0:1]
        pay[1, x : x + 1, :] = total[1:2]
        pay[2, x : x + 1, :] = total[2:3]
        pay[3, x : x + 1, :] = total[3:4] + total[4:5]
    flip = flip_matrix(up, cells_y)
    fx = jnp.concatenate([out_row[0], out_row[1], jnp.zeros((6, cells_y), F32)], axis=0)
    turned = nt(stacked(fx), flip.astype(BF16))
    pay[4] = turned[0:8] + turned[8:16] + turned[16:24]
    for sign in range(2):
        total = jnp.zeros((cells_x, LANES), F32)
        for at in range(count // LANES):
            _, iy = lane_ints(first_ky, sign, at * LANES, (cells_x, LANES))
            total += jnp.abs(iy).astype(F32) * edge[sign][:cells_x, at * LANES : (at + 1) * LANES]
        pay[6 - sign] = total
        ymsg[sign] = edge[sign][:cells_x].astype(BF16)
    for copy in small:
        copy.wait()


def newton_params(u0, u1, u2, u3):
    ux, uy = u1 / u0, u2 / u0
    square = ux * ux + uy * uy
    temperature = u3 / u0 - square / 2.0
    p = [jnp.log(u0 / temperature) - square / (2.0 * temperature), ux / temperature, uy / temperature, -1.0 / temperature]
    last = (HALF - 0.5) * STEP
    for _ in range(NEWTON):
        half_p3 = p[3] * 0.5
        sums, tops = [], []
        for slope in (p[1], p[2]):
            vertex = jnp.where(p[3] < 0.0, -slope / p[3], 0.0) * (1.0 / STEP)
            node = (jnp.clip(jnp.floor(vertex), -HALF, HALF - 1.0) + 0.5) * STEP
            end = (last * last) * half_p3 + last * jnp.abs(slope)
            top = jnp.maximum(node * (slope + node * half_p3), end)
            total = [None] * 5
            for i in range(HALF):
                value = (i + 0.5) * STEP
                even, odd = (value * value) * half_p3 - top, value * slope
                plus, minus = jnp.exp(even + odd), jnp.exp(even - odd)
                even, odd = plus + minus, plus - minus
                terms = [even, value * odd, value**2 * even, value**3 * odd, value**4 * even]
                total = [t if old is None else old + t for old, t in zip(total, terms)]
            sums.append(total)
            tops.append(top)
        scale = jnp.exp(p[0] + (tops[0] + tops[1])) * WEIGHT
        x = sums[0]
        y = [scale * t for t in sums[1]]
        x2, y2 = x[2] * y[0], x[0] * y[2]
        n = [x[0] * y[0], x[1] * y[0], x[0] * y[1], (x2 + y2) * 0.5, x2, x[1] * y[1],
             (x[3] * y[0] + x[1] * y[2]) * 0.5, y2, (x[2] * y[1] + x[0] * y[3]) * 0.5,
             (x[4] * y[0] + 2.0 * (x[2] * y[2]) + x[0] * y[4]) * 0.25]
        layout = [[0, 1, 2, 3], [1, 4, 5, 6], [2, 5, 7, 8], [3, 6, 8, 9]]
        matrix = [[n[layout[r][c]] for c in range(4)] for r in range(4)]
        target = [n[0] - u0, n[1] - u1, n[2] - u2, n[3] - u3]
        for pivot in range(4):
            for lower in range(pivot + 1, 4):
                factor = matrix[lower][pivot] / matrix[pivot][pivot]
                for col in range(pivot, 4):
                    matrix[lower][col] = matrix[lower][col] - factor * matrix[pivot][col]
                target[lower] = target[lower] - factor * target[pivot]
        result = [None] * 4
        for pivot in (3, 2, 1, 0):
            accum = target[pivot]
            for col in range(pivot + 1, 4):
                accum = accum - matrix[pivot][col] * result[col]
            result[pivot] = accum / matrix[pivot][pivot]
        p = [a - b for a, b in zip(p, result)]
    return p


def block_speeds(first_ky, block, per_sign, shape):
    ix, iy = lane_ints(first_ky, block // per_sign, (block % per_sign) * LANES, shape)
    return jnp.abs(ix).astype(F32) * UNIT, jnp.abs(iy).astype(F32) * UNIT


def fill_inflow(info, ky, same, other, g, xin, yin, xw, yw, kx):
    blocks, slots, padded, _ = g.shape
    cells_x, cells_y = slots - 1, padded - 8
    per_sign = blocks // 2
    first_ky = info[0]
    anti = flip_matrix(False, cells_y)
    turned = nn(stacked(other[0]), anti.astype(BF16))
    fx = (same[0] + (turned[0:8] + turned[8:16] + turned[16:24])) * FLUX_SCALE
    lane = iota((24, 2 * LANES), 1) // LANES
    columns = tn(stacked(fx), (iota((24, 2 * LANES), 0) % 8 == 1 - lane).astype(F32).astype(BF16))
    fy = jnp.sum(other[1], axis=1, keepdims=True) + reverse_rows(jnp.sum(other[2], axis=1, keepdims=True))
    fy = fy * FLUX_SCALE
    fy = [reverse_rows(fy), fy]
    y_wall = info[4] == 1
    for sign in range(2):
        column = columns[:, sign * LANES : (sign + 1) * LANES]
        x_wall = info[3 - sign] == 1
        fy_wide = jnp.broadcast_to(fy[sign], (cells_x, LANES))
        for at in range(per_sign):
            block = sign * per_sign + at
            ix, iy = lane_ints(first_ky, sign, at * LANES, (8, LANES))
            maxwell = jnp.exp((ix * ix + iy * iy).astype(F32) * (-UNIT * UNIT / 2.0))
            ghost = jnp.where(kx[sign] == 1.0, xw[block], column * maxwell[0:1])
            g[block, 0, 8:, :] = jnp.where(x_wall, ghost, xin(block))
            ghost_y = jnp.where(ky[sign] == 1.0, yw[block], fy_wide * maxwell)
            value = jnp.where(y_wall, ghost_y, yin(block))
            for x in range(cells_x):
                g[block, 1 + x, 7:8, :] = value[x : x + 1]


def sweep(info, g, s, r, part="all"):
    blocks, slots, padded, _ = g.shape
    cells_x, cells_y = slots - 1, padded - 8
    tile = 16
    inner = [(x, at) for x in range(cells_x - 1, 0, -1) for at in range(cells_y - tile, 0, -tile)]
    rim = [(x, 0) for x in range(cells_x - 1, 0, -1)] + [(0, at) for at in range(cells_y - tile, -1, -tile)]
    todo = inner if part == "inner" else rim if part == "rim" else inner + rim

    def step(both, carry):
        for i in range(2):
            block = 2 * both + i
            half = slice(i * LANES, (i + 1) * LANES)
            ax, ay = block_speeds(info[0], block, blocks // 2, (tile, LANES))
            for x, at in todo:
                here = pl.ds(at, tile)
                value = s[block, x, here, :] + ax * g[block, x, pl.ds(8 + at, tile), :]
                value += ay * g[block, 1 + x, pl.ds(7 + at, tile), :]
                value = (value * r[both, x, here, half]).astype(BF16)
                g[block, 1 + x, pl.ds(8 + at, tile), :] = value.astype(F32)
        return carry

    lax.fori_loop(0, blocks // 2, step, 0)


def inner_kernel(s, r, g_in, g):
    blocks = g.shape[0]
    sweep(device_info(blocks // 2 * LANES // HALF), g, s, r, "inner")


def send_out(info, g, xmsg, ymsg, flux):
    blocks, slots, padded, _ = g.shape
    cells_x, cells_y = slots - 1, padded - 8
    per_sign = blocks // 2
    fx = None
    for sign in range(2):
        total = jnp.zeros((cells_y, LANES), F32)
        total_y = jnp.zeros((cells_x, LANES), F32)
        for at in range(per_sign):
            block = sign * per_sign + at
            ix, iy = lane_ints(info[0], sign, at * LANES, (8, LANES))
            ix, iy = jnp.abs(ix).astype(F32), jnp.abs(iy).astype(F32)
            row = g[block, cells_x, 8:, :]
            total += row * ix[0:1]
            edge = jnp.concatenate([g[block, 1 + x, padded - 1 : padded, :] for x in range(cells_x)], axis=0)
            ymsg[block] = edge.astype(BF16)
            total_y += edge * iy
        for at in range(per_sign):
            take = sign * (1 - info[5]) + (1 - sign) * info[5]
            xmsg[sign][at] = g[take * per_sign + at, cells_x, 8:, :].astype(BF16)
        pick = (iota((16, 3 * LANES), 0) == sign).astype(F32).astype(BF16)
        part = nt(pick, jnp.concatenate(pieces(total), axis=1).astype(BF16))[0:8]
        fx = part if fx is None else fx + part
        flux[2 - sign] = total_y
    flux[0] = fx


def spread(table, choice, size):
    row = iota((3 * size, choice.shape[1]), 0) % size
    return nn(table, (row == choice).astype(F32).astype(BF16))


def transposed(flip, table, ref, x, cells_x, cells_y):
    wide = nt(flip, stacked(table)).astype(BF16)
    ref[1, x * cells_y : (x + 1) * cells_y, :] = wide
    ref[0, (cells_x - 1 - x) * cells_y : (cells_x - x) * cells_y, :] = wide


def table_kernel(relax, kindx, kindy, pt, lri, bti, g, r, xw, yw, kx, ky, tr):
    cells_x, _, count, cells_y = pt.shape
    per_sign = count // LANES
    info = device_info(count // HALF)
    flip = flip_matrix(info[1] == 1, cells_y).astype(BF16)
    base = 1.0 / TIME_STEP + 1.0 / relax[...]
    steps = iota((NVX, cells_y), 0).astype(F32) * STEP
    for x in range(cells_x):
        transposed(flip, 1.0 / (base[x : x + 1] + steps), tr, x, cells_x, cells_y)
    kind = jnp.concatenate([kindx[1:2], kindx[0:1], jnp.zeros((6, cells_y), jnp.int32)], axis=0).astype(F32)
    kind = nt(kind.astype(BF16), flip).astype(BF16)
    sides = jnp.concatenate([kindy[...].astype(F32), jnp.zeros((6, cells_x), F32)], axis=0).astype(BF16)
    for sign in range(2):
        row, col = iota((16, cells_x), 0), iota((16, cells_x), 1)
        order = (col == (row if sign else cells_x - 1 - row)).astype(F32).astype(BF16)
        pick = (iota((8, LANES), 0) == 1 - info[1]).astype(F32).astype(BF16)
        ky[sign] = nn(nt(order, sides).astype(BF16), pick)[:cells_x]
        kx[sign] = tn(kind, (iota((8, LANES), 0) == sign).astype(F32).astype(BF16))
        for at in range(per_sign):
            block = sign * per_sign + at
            chunk = [2 * ((at * (LANES // HALF) + i) * NVX + HALF * sign) for i in range(LANES // HALF)]
            part = jnp.concatenate([lri[c : c + 2 * HALF, :] for c in chunk], axis=0)
            pick = (iota((LANES, 2 * LANES), 1) == 2 * iota((LANES, 2 * LANES), 0) + 1 - sign).astype(F32).astype(BF16)
            xw[block] = nt(flip, nn(pick, part).astype(BF16))
            part = nn(order, bti[1 - info[1], :, at * 2 * LANES : (at + 1) * 2 * LANES]).astype(BF16)
            row, col = iota((2 * LANES, LANES), 0), iota((2 * LANES, LANES), 1)
            pick = (row == col // HALF * NVX + HALF * sign + col % HALF).astype(F32).astype(BF16)
            yw[block] = nn(part, pick)[:cells_x]
        for at in range(0, per_sign, 2):
            ix, iy = lane_ints(info[0], sign, at * LANES, (1, 2 * LANES))
            both = (sign * per_sign + at) // 2
            r[both] = spread(tr[sign], (jnp.abs(ix) + jnp.abs(iy)) // 2, NVX).reshape(cells_x, cells_y, 2 * LANES)
            for xt in range(cells_x):
                x = xt if sign else cells_x - 1 - xt
                value = nt(flip, pt[x, sign, at * LANES : (at + 2) * LANES, :])
                for i in range(2):
                    g[2 * both + i, 1 + xt, 8:, :] = value[:, i * LANES : (i + 1) * LANES]


def first_kernel(ky, same, other, relax, pair0, pair1, yrecv, xw, yw, kx, r, g_in,
                 g, s, xmsg0, xmsg1, ymsg, flux, ta, tb, fa, fb):
    blocks, slots, padded, _ = g.shape
    cells_x, cells_y = slots - 1, padded - 8
    per_sign = blocks // 2
    local_ky = per_sign * LANES // HALF
    info = device_info(local_ky)
    first_ky, up = info[0], info[1] == 1
    total = [same[q] + other[q] for q in range(4)]
    p = newton_params(total[0] * WEIGHT, total[1] * (WEIGHT * UNIT), total[2] * (WEIGHT * UNIT),
                      total[3] * (WEIGHT * UNIT * UNIT / 2.0))
    lead = p[0] - jnp.log(relax[...])
    flip = flip_matrix(up, cells_y).astype(BF16)
    vx = (2 * iota((NVX, cells_y), 0) - (NVX - 1)).astype(F32) * UNIT
    vy = (2 * (first_ky + iota((local_ky, cells_y), 0)) - (NVX - 1)).astype(F32) * UNIT
    half_p3 = p[3] * 0.5
    for x in range(cells_x):
        here = slice(x, x + 1)
        arg = vy * (p[2][here] + vy * half_p3[here])
        top = jnp.max(arg, axis=0, keepdims=True)
        transposed(flip, jnp.exp(arg - top), tb, x, cells_x, cells_y)
        arg = (lead[here] + top) + vx * (p[1][here] + vx * half_p3[here])
        transposed(flip, jnp.exp(arg), ta, x, cells_x, cells_y)
    for sign in range(2):
        fa[...] = spread(ta[sign], iota((1, LANES), 1) % HALF + HALF * sign, NVX)
        for at in range(0, per_sign, 2):
            block = sign * per_sign + at
            fb[...] = spread(tb[sign], iota((1, 2 * LANES), 1) // HALF + at * (LANES // HALF), local_ky)
            for xt in range(cells_x):
                here = slice(xt * cells_y, (xt + 1) * cells_y)
                for i in range(2):
                    maxwell = fa[here, :] * fb[here, i * LANES : (i + 1) * LANES]
                    s[block + i, xt] = g[block + i, 1 + xt, 8:, :] * (1.0 / TIME_STEP) + maxwell

    def xin(block):
        at = block % per_sign
        first = (info[5] == 1) == (block < per_sign)
        here = slice(at * LANES, (at + 1) * LANES)
        return nt(flip, jnp.where(first, pair0[here, :], pair1[here, :]))

    def yin(block):
        at = block % per_sign
        return yrecv[block // per_sign, :, at * LANES : (at + 1) * LANES].astype(F32)

    fill_inflow(info, ky, same.at[4:7], other.at[4:7], g, xin, yin, xw, yw, kx)
    sweep(info, g, s, r)
    send_out(info, g, (xmsg0, xmsg1), ymsg, flux)


def next_kernel(last, ky, same, other, pair0, pair1, yrecv, xw, yw, kx, s, r, g_in, *outs):
    blocks, slots, padded, _ = g_in.shape
    per_sign = blocks // 2
    info = device_info(per_sign * LANES // HALF)
    if last:
        out, g, rows, staged, sems = outs
    else:
        g, xmsg0, xmsg1, ymsg, flux = outs

    def xin(block):
        first = (info[5] == 1) == (block < per_sign)
        return jnp.where(first, pair0[block % per_sign].astype(F32), pair1[block % per_sign].astype(F32))

    def yin(block):
        return yrecv[block].astype(F32)

    fill_inflow(info, ky, same, other, g, xin, yin, xw, yw, kx)
    sweep(info, g, s, r, "rim")
    if not last:
        send_out(info, g, (xmsg0, xmsg1), ymsg, flux)
        return
    cells_x, cells_y = slots - 1, padded - 8
    flip = flip_matrix(info[1] == 1, cells_y).astype(BF16)

    span = HALF * cells_x
    copies = []
    for sign in range(2):
        for at in range(per_sign):
            for x in range(cells_x):
                xt = x if sign else cells_x - 1 - x
                value = g[sign * per_sign + at, 1 + xt, 8:, :].astype(BF16)
                rows[pl.ds(x, LANES, stride=cells_x), :] = tn(value, flip)
            for i in range(LANES // HALF):
                chunk = (at * (LANES // HALF) + i) * 2 + sign
                staged[chunk * span : (chunk + 1) * span, :] = rows[i * span : (i + 1) * span, :].astype(BF16)
                copies.append(pltpu.make_async_copy(
                    staged.at[pl.ds(chunk * span, span), :], out.at[pl.ds(chunk * span, span), :], sems.at[chunk]))
                copies[-1].start()
    for copy in copies:
        copy.wait()


def call(kernel, outs, ins, smem=(), scratch=(), aliases=None, mib=20, far_in=(), far_out=(), cost=None):
    here = pl.BlockSpec(memory_space=pltpu.VMEM)
    scalar = pl.BlockSpec(memory_space=pltpu.SMEM)
    far = pl.BlockSpec(memory_space=pltpu.HBM)
    return pl.pallas_call(
        kernel,
        out_shape=outs,
        in_specs=[scalar if i in smem else far if i in far_in else here for i in range(len(ins))],
        out_specs=tuple(far if i in far_out else here for i in range(len(outs))),
        scratch_shapes=list(scratch),
        input_output_aliases=aliases or {},
        cost_estimate=cost,
        compiler_params=pltpu.CompilerParams(vmem_limit_bytes=mib << 20),
    )(*ins)


def body(previous, relax_time, left_right_kind, bottom_top_kind, left_right_inflow, bottom_top_inflow):
    vel_rows, cells_x, cells_y = previous.shape
    local_ky = vel_rows // NVX
    count = local_ky * HALF
    per_sign = count // LANES
    blocks = 2 * per_sign
    nvel, ngx, ngy = lax.axis_size("vel"), lax.axis_size("gx"), lax.axis_size("gy")

    def pairs(count, start):
        low = range(start, count - 1, 2)
        return [(i, i + 1) for i in low] + [(i + 1, i) for i in low]

    def exchange(first, second, edge, part):
        reach = 1
        while reach < nvel // 2:
            part = part + lax.ppermute(part, "vel", [(i, i ^ reach) for i in range(nvel)])
            reach *= 2
        other = lax.ppermute(part, "vel", [(i, i ^ reach) for i in range(nvel)])
        edge = lax.ppermute(edge, "gy", pairs(ngy, 0))
        first = lax.ppermute(first, "gx", pairs(ngx, 0))
        second = lax.ppermute(second, "gx", pairs(ngx, 1))
        return (first, second), edge, (part, other)

    assert ngy == 2 and nvel & (nvel - 1) == 0, "mesh shape"
    sds = jax.ShapeDtypeStruct
    staging = [pltpu.VMEM((LANES * cells_x + cells_x, cells_y), F32), pltpu.VMEM((vel_rows * cells_x, cells_y), BF16),
               pltpu.SemaphoreType.DMA((vel_rows // HALF,))]

    def far(a):
        return pltpu.with_memory_space_constraint(a, pltpu.HBM)

    pay, ymsg, pt, xmsg0, xmsg1, relax, kindx, kindy, lri, bti = call(
        moments_kernel,
        (sds((7, 8, LANES), F32), sds((2, cells_x, count), BF16), sds((cells_x, 2, count, cells_y), BF16),
         sds((count, cells_y), BF16), sds((count, cells_y), BF16), sds(relax_time.shape, F32), sds(left_right_kind.shape, jnp.int32), sds(bottom_top_kind.shape, jnp.int32),
         sds((2 * vel_rows, cells_y), BF16), sds((2, cells_x, vel_rows), BF16)),
        (far(previous.reshape(vel_rows * cells_x, cells_y)), far(relax_time), far(left_right_kind), far(bottom_top_kind),
         far(left_right_inflow.reshape(2 * vel_rows, cells_y)), far(bottom_top_inflow.transpose(1, 2, 0))),
        scratch=staging + [pltpu.SemaphoreType.DMA((5,))], mib=10, far_in=(0, 1, 2, 3, 4, 5))
    halo, yrecv, sums = exchange(xmsg0, xmsg1, ymsg, pay)
    g_shape = sds((blocks, cells_x + 1, cells_y + 8, LANES), F32)
    full = sds((blocks, cells_x, cells_y, LANES), F32)
    wide = sds((blocks // 2, cells_x, cells_y, 2 * LANES), F32)
    messages = (sds((per_sign, cells_y, LANES), BF16), sds((per_sign, cells_y, LANES), BF16),
                sds((blocks, cells_x, LANES), BF16), sds((3, 8, LANES), F32))
    work = pl.CostEstimate(flops=8 * vel_rows * cells_x * cells_y, bytes_accessed=16 * vel_rows * cells_x * cells_y, transcendentals=0)
    g, r, xw, yw, kx, ky = call(
        table_kernel,
        (g_shape, wide, sds((blocks, cells_y, LANES), F32), sds((blocks, cells_x, LANES), F32), sds((2, cells_y, LANES), F32),
         sds((2, cells_x, LANES), F32)),
        (relax, kindx, kindy, pt, lri, bti),
        scratch=[pltpu.VMEM((2, cells_x * cells_y, 3 * NVX), BF16)], mib=22, cost=work)
    g, s, xmsg0, xmsg1, ymsg, flux = call(
        first_kernel,
        (g_shape, full) + messages,
        (ky, *sums, relax, *halo, yrecv, xw, yw, kx, r, g), aliases={11: 0},
        scratch=[
            pltpu.VMEM((2, cells_x * cells_y, 3 * NVX), BF16), pltpu.VMEM((2, cells_x * cells_y, 3 * local_ky), BF16),
            pltpu.VMEM((cells_x * cells_y, LANES), F32), pltpu.VMEM((cells_x * cells_y, 2 * LANES), F32)], mib=24)
    for number in range(1, SWEEPS):
        halo, yrecv, sums = exchange(xmsg0, xmsg1, ymsg, flux)
        g = call(inner_kernel, (g_shape,), (s, r, g), aliases={2: 0}, mib=20, cost=work)[0]
        ins = (ky, *sums, *halo, yrecv, xw, yw, kx, s, r, g)
        if number == SWEEPS - 1:
            out, _ = call(functools.partial(next_kernel, True),
                          (sds((vel_rows * cells_x, cells_y), BF16), g_shape), ins, aliases={11: 1},
                          scratch=staging, mib=22, far_out=(0,))
        else:
            g, xmsg0, xmsg1, ymsg, flux = call(
                functools.partial(next_kernel, False), (g_shape,) + messages, ins, aliases={11: 0}, mib=22)
    return out.reshape(vel_rows, cells_x, cells_y)


def solution(mesh):
    return jax.shard_map(
        body,
        mesh=mesh,
        in_specs=(P("vel", "gx", "gy"), P("gx", "gy"), P(None, "gy"), P(None, "gx"), P("vel", None, "gy"), P("vel", None, "gx")),
        out_specs=P("vel", "gx", "gy"),
        check_vma=False,
    )
```
